512 devices in a mesh: wide: 64 (over y, x, z_hi), narrow: 8 (over z_lo, core).
Axes of the slice: x: 4, y: 8, z: 8 (z_hi: 2, z_lo: 4; z = z_hi * 4 + z_lo), core: 2. Of those that a mesh axis runs over, the one named last changes fastest.
Arguments:
- context: bfloat16 [65536, 3072], P('wide', 'narrow'), may hold values from -6 to 6
- out_weight: bfloat16 [3072, 6144], P('wide', 'narrow'), may hold values from -0.109375 to 0.109375
- residual: bfloat16 [65536, 6144], P('wide', 'narrow'), may hold values from -180 to 180
- ln_gain: bfloat16 [6144], P('narrow'), may hold values from 0.5 to 1.5
- side_down: bfloat16 [6144, 768], P('narrow', 'wide'), may hold values from -0.078125 to 0.078125
- f_weight: bfloat16 [384, 384], replicated, may hold values from -0.3125 to 0.3125
- g_weight: bfloat16 [384, 384], replicated, may hold values from -0.3125 to 0.3125
- targets: float32 [65536, 768], P(('wide', 'narrow')), may hold values from -18 to 18
Outputs:
- side_out: float32 [65536, 768], P(('wide', 'narrow'))
- f_grad: float32 [384, 384], replicated
- g_grad: float32 [384, 384], replicated
The draws below stay inside these ranges and needn't reach their ends.
All inputs are finite; a program needn't handle non-finite values.
Results may differ from the reference program's by a relative error of at most 0.00035.
The reference program's roundings to bfloat16 on the way (of `stream` and `scaled`) count: a program that leaves them out, or rounds other values in their place, can miss the bound.
Values may be sent and summed in bfloat16 or wider, within the bound.
A program may use at most 64 MiB of HBM per device.

```python
import math
import jax
import jax.numpy as jnp
from jax import lax

D = 6144
SIDE = 768
HD = 3072
HALF = 384
TOKENS = 65536


def draw_targets(key, part):
    first_key = jax.random.fold_in(key, 11)
    position = jnp.arange(TOKENS, dtype=jnp.float32) / max(TOKENS - 1, 1)
    rising = jnp.exp(position * jnp.log(3.0))
    base = jnp.clip(jax.random.normal(first_key, (TOKENS, SIDE), jnp.float32), -6.0, 6.0)
    return (base * rising[:, None]).astype(jnp.float32)


def draw_residual(key, part):
    noise_key = jax.random.fold_in(key, 31)
    row_key = jax.random.fold_in(key, 37)
    column_key = jax.random.fold_in(key, 41)
    shift_key = jax.random.fold_in(key, 43)
    feature = jnp.arange(D, dtype=jnp.float32) / max(D - 1, 1)
    rise = jnp.exp(feature * 0.6 * math.log(3.0))
    row_scale = jnp.exp(jax.random.uniform(row_key, (TOKENS,), jnp.float32, math.log(0.3), math.log(3.0)))
    noise = jnp.clip(jax.random.normal(noise_key, (TOKENS, D), jnp.float32), -4.0, 4.0)
    column_scale = jnp.exp(jax.random.uniform(column_key, (D,), jnp.float32, math.log(0.3), math.log(3.0))) * rise
    shift = jnp.clip(jax.random.normal(shift_key, (TOKENS,), jnp.float32), -2.5, 2.5)
    values = row_scale[:, None] * column_scale[None, :] * (noise + shift[:, None])
    return values.astype(jnp.bfloat16)


def block_scale(rng, shape, cuts, least, largest):
    factor_of, own = 1.0, jax.random.fold_in(rng, 6)
    for axis_at, blocks in cuts:
        steps = jnp.exp(jax.random.uniform(jax.random.fold_in(own, axis_at), (blocks,), jnp.float32, least / len(cuts), largest / len(cuts)))
        factor_of = factor_of * jnp.repeat(steps, shape[axis_at] // blocks).reshape([-1 if axis == axis_at else 1 for axis in range(len(shape))])
    return factor_of


def scatter_about(key, dims, width, reach, shards=(), kind=jnp.bfloat16):
    factor_of = block_scale(key, dims, shards, -0.22, 0.18) if shards else 1.0
    array = jax.random.normal(key, dims, jnp.float32) * width * factor_of
    return jnp.minimum(jnp.maximum(array, -reach), reach).astype(kind)


def setup_inputs(seed: int = 0) -> dict:
    seeds = jax.random.split(jax.random.key(seed), 9)
    context = scatter_about(seeds[0], (TOKENS, HD), 1.0, 6.0, ((0, 64), (1, 8)))
    out_weight = scatter_about(seeds[1], (HD, D), HD ** -0.5, 0.109375, ((0, 64), (1, 8)))
    residual = draw_residual(jax.random.fold_in(seeds[8], 71), 0)
    ln_gain = jnp.clip(1.0 + 0.1 * jax.random.normal(seeds[3], (D,), jnp.float32), 0.5, 1.5).astype(jnp.bfloat16)
    side_down = scatter_about(seeds[4], (D, SIDE), D ** -0.5, 0.078125, ((0, 8), (1, 64)))
    f_weight = scatter_about(seeds[5], (HALF, HALF), HALF ** -0.5, 0.3125)
    g_weight = scatter_about(seeds[6], (HALF, HALF), HALF ** -0.5, 0.3125)
    targets = draw_targets(jax.random.fold_in(seeds[8], 71), 0)
    return dict(context=context, out_weight=out_weight, residual=residual, ln_gain=ln_gain, side_down=side_down, f_weight=f_weight, g_weight=g_weight, targets=targets)


def coupling(values, weight):
    return jax.nn.gelu(jnp.dot(values, weight, precision=lax.Precision.HIGHEST))

def side_block(f_w, g_w, side_in):
    half = side_in.shape[1] // 2
    first = side_in[:, :half]
    second = side_in[:, half:]
    upper = first + coupling(second, f_w)
    lower = second + coupling(upper, g_w)
    return jnp.concatenate([upper, lower], axis=1)

def reference(context, out_weight, residual, ln_gain, side_down, f_weight, g_weight, targets):
    block_rows = min(1024, TOKENS)
    blocks = TOKENS // block_rows
    ctx_blocks = context.reshape(blocks, block_rows, context.shape[1])
    res_blocks = residual.reshape(blocks, block_rows, residual.shape[1])
    gain_value = ln_gain.astype(jnp.float32)
    gain_map = jnp.dot(ln_gain[None, :], side_down, preferred_element_type=jnp.float32)[0]

    def one_block(pair):
        ctx, res = pair
        attn_out = jnp.dot(ctx, out_weight, preferred_element_type=jnp.float32)
        stream = (res.astype(jnp.float32) + attn_out).astype(jnp.bfloat16)
        stream_value = stream.astype(jnp.float32)
        row_sum = lax.optimization_barrier(jnp.sum(stream_value, axis=1))
        row_squares = lax.optimization_barrier(jnp.sum(stream_value * stream_value, axis=1))
        scaled = (stream_value * gain_value[None, :]).astype(jnp.bfloat16)
        projected = jnp.dot(scaled, side_down, preferred_element_type=jnp.float32)
        mean = row_sum / D
        spread = row_squares / D - mean * mean
        return (projected - mean[:, None] * gain_map[None, :]) / jnp.sqrt(spread + 1e-06)[:, None]
    side_in = lax.map(one_block, (ctx_blocks, res_blocks)).reshape(TOKENS, side_down.shape[1])
    f_w = f_weight.astype(jnp.float32)
    g_w = g_weight.astype(jnp.float32)

    def loss_of(fw_value, gw_value):
        out = side_block(fw_value, gw_value, side_in)
        return 0.5 * jnp.sum((out - targets) ** 2) / TOKENS
    side_out = side_block(f_w, g_w, side_in)
    f_grad, g_grad = jax.grad(loss_of, argnums=(0, 1))(f_w, g_w)
    return (side_out, f_grad, g_grad)
```

```python
import jax
import jax.numpy as jnp
from jax import lax
from jax.experimental import pallas as pl
from jax.experimental.pallas import tpu as pltpu
from jax.sharding import PartitionSpec as P

MESH = pl.DeviceIdType.MESH


def position():
    w = lax.axis_index("wide")
    n = lax.axis_index("narrow")
    return w // 8, (w // 2) % 4, (w % 2) * 4 + n // 2, n % 2


def device(y, x, z, c):
    return ((y * 4 + x) * 2 + z // 4, (z % 4) * 2 + c)


def ar_kernel(f_ref, g_ref, f_out, g_out, buf0, half, buf_a, mid, buf_b, buf_x, tail, fin, sems_s, sems_r):
    y, x, z, c = position()
    on_z = 1 - c
    pos_a = z * on_z + y * c
    pos_b = y * on_z + z * c

    def along_a(d):
        return device((y + d * c) % 8, x, (z + d * on_z) % 8, c)

    def along_b(d):
        return device((y + d * on_z) % 8, x, (z + d * c) % 8, c)

    def along_x(d):
        return device(y, (x + d) % 4, z, c)

    sibling = device(y, x, z, 1 - c)
    barrier = pltpu.get_barrier_semaphore()
    partners = [sibling] + [along_a(d) for d in range(1, 8)] + [along_b(d) for d in range(1, 8)] + [along_x(d) for d in range(1, 4)]
    for partner in partners:
        pl.semaphore_signal(barrier, inc=1, device_id=partner, device_id_type=MESH)
    pl.semaphore_wait(barrier, len(partners))
    sent = []

    def send(src, dst, slot, to):
        copy = pltpu.make_async_remote_copy(
            src_ref=src, dst_ref=dst, send_sem=sems_s.at[slot], recv_sem=sems_r.at[slot], device_id=to, device_id_type=MESH
        )
        copy.start()
        sent.append(copy)
        return copy

    def own(total, mine):
        copy = pltpu.make_async_remote_copy(
            src_ref=mine, dst_ref=buf0, send_sem=sems_s.at[0], recv_sem=sems_r.at[0], device_id=sibling, device_id_type=MESH
        )
        copy.start()
        copy.wait()
        half[...] = total[...] + buf0[...]

    @pl.when(c == 0)
    def _():
        own(f_ref, g_ref)

    @pl.when(c == 1)
    def _():
        own(g_ref, f_ref)

    def rows(ref, at, n):
        return ref.at[pl.ds(pl.multiple_of(at * n, 8), n)]

    copies = [
        send(rows(half, (pos_a + d) % 8, 48), buf_a.at[d - 1], d, along_a(d)) for d in range(1, 8)
    ]
    total = half[pl.ds(pl.multiple_of(pos_a * 48, 8), 48), :]
    for d in range(1, 8):
        copies[d - 1].wait_recv()
        total = total + buf_a[d - 1]
    mid[0:48, :] = total
    mid[48:64, :] = jnp.zeros((16, 384), jnp.float32)
    copies = [
        send(rows(mid, (pos_b + d) % 8, 8), buf_b.at[d - 1], 7 + d, along_b(d)) for d in range(1, 8)
    ]
    total = mid[pl.ds(pl.multiple_of(pos_b * 8, 8), 8), :]
    for d in range(1, 8):
        copies[d - 1].wait_recv()
        total = total + buf_b[d - 1]
    buf_x[x] = total
    copies = [send(buf_x.at[x], buf_x.at[x], 14 + d, along_x(d)) for d in range(1, 4)]
    for copy in copies:
        copy.wait_recv()
    tail[pl.ds(pl.multiple_of(pos_b * 8, 8), 8), :] = (buf_x[0] + buf_x[1]) + (buf_x[2] + buf_x[3])
    copies = [send(rows(tail, pos_b, 8), rows(tail, pos_b, 8), 17 + d, along_b(d)) for d in range(1, 8)]
    for copy in copies:
        copy.wait_recv()
    place = pl.ds(pl.multiple_of(pos_a * 48, 8), 48)
    copies = [send(tail.at[pl.ds(0, 48)], fin.at[c, place], 24 + d, along_a(d)) for d in range(1, 8)]
    shares = [send(tail.at[pl.ds(0, 48)], fin.at[c, place], 32, sibling)]
    fin[c, place, :] = tail[0:48, :]
    for d in range(1, 8):
        copies[d - 1].wait_recv()
        there = pl.ds(pl.multiple_of((pos_a + 8 - d) % 8 * 48, 8), 48)
        shares.append(send(fin.at[c, there], fin.at[c, there], 32 + d, sibling))
    for copy in shares:
        copy.wait_recv()
    f_out[...] = fin[0]
    g_out[...] = fin[1]
    for copy in sent:
        copy.wait_send()


def all_reduce(f_local, g_local):
    size = f_local.shape[0]
    vmem = pl.BlockSpec(memory_space=pltpu.VMEM)
    full = jax.ShapeDtypeStruct((size, size), jnp.float32)
    return pl.pallas_call(
        ar_kernel,
        out_shape=(full, full),
        in_specs=[vmem, vmem],
        out_specs=(vmem, vmem),
        scratch_shapes=[
            pltpu.VMEM((size, size), jnp.float32),
            pltpu.VMEM((size, size), jnp.float32),
            pltpu.VMEM((7, size // 8, size), jnp.float32),
            pltpu.VMEM((64, size), jnp.float32),
            pltpu.VMEM((7, 8, size), jnp.float32),
            pltpu.VMEM((4, 8, size), jnp.float32),
            pltpu.VMEM((64, size), jnp.float32),
            pltpu.VMEM((2, size, size), jnp.float32),
            pltpu.SemaphoreType.DMA((40,)),
            pltpu.SemaphoreType.DMA((40,)),
        ],
        compiler_params=pltpu.CompilerParams(collective_id=1, has_side_effects=True),
        name="gradient_sum",
    )(f_local, g_local)


def coupling(values, weight):
    return jax.nn.gelu(jnp.dot(values, weight, precision=lax.Precision.HIGHEST))


def per_device(context, out_weight, residual, ln_gain, side_down, f_weight, g_weight, targets):
    full_weight = lax.all_gather(out_weight, "wide", axis=0, tiled=True)
    whole = lax.all_gather(context, "narrow", axis=1, tiled=True)
    attn_sum = jnp.dot(whole, full_weight, preferred_element_type=jnp.float32)
    stream = (residual.astype(jnp.float32) + attn_sum).astype(jnp.bfloat16)
    stream_value = stream.astype(jnp.float32)
    row_sum = jnp.sum(stream_value, axis=1)
    row_squares = jnp.sum(stream_value * stream_value, axis=1)
    scaled = (stream_value * ln_gain.astype(jnp.float32)[None, :]).astype(jnp.bfloat16)
    down_full = lax.all_gather(side_down, "wide", axis=1, tiled=True)
    gain_part = jnp.dot(ln_gain[None, :], down_full, preferred_element_type=jnp.float32)[0]
    local_rows = targets.shape[0]
    sums_all, squares_all, gain_map = lax.psum((row_sum, row_squares, gain_part), "narrow")
    offset = lax.axis_index("narrow") * local_rows
    token_sum = lax.dynamic_slice_in_dim(sums_all, offset, local_rows, 0)
    token_squares = lax.dynamic_slice_in_dim(squares_all, offset, local_rows, 0)
    projected = lax.psum_scatter(
        jnp.dot(scaled, down_full, preferred_element_type=jnp.float32),
        "narrow",
        scatter_dimension=0,
        tiled=True,
    )
    features = stream.shape[1] * lax.axis_size("narrow")
    mean = token_sum / features
    spread = token_squares / features - mean * mean
    side_in = (projected - mean[:, None] * gain_map[None, :]) / jnp.sqrt(spread + 1e-06)[:, None]
    half = side_in.shape[1] // 2
    f_w = f_weight.astype(jnp.float32)
    g_w = g_weight.astype(jnp.float32)
    first = side_in[:, :half]
    second = side_in[:, half:]
    upper = first + coupling(second, f_w)
    g_value, g_pull = jax.vjp(coupling, upper, g_w)
    lower = second + g_value
    side_out = jnp.concatenate([upper, lower], axis=1)
    all_tokens = local_rows * lax.axis_size("wide") * lax.axis_size("narrow")
    misfit = (side_out - targets) / all_tokens
    upper_back, g_local = g_pull(misfit[:, half:])
    rebuilt = lower - g_value
    upper_total = misfit[:, :half] + upper_back
    f_value, f_pull = jax.vjp(coupling, rebuilt, f_w)
    f_local = f_pull(upper_total)[1]
    f_total, g_total = all_reduce(f_local, g_local)
    return (side_out, f_total, g_total)


def solution(mesh):
    in_specs = (
        P("wide", "narrow"),
        P("wide", "narrow"),
        P("wide", "narrow"),
        P("narrow"),
        P("narrow", "wide"),
        P(),
        P(),
        P(("wide", "narrow"), None),
    )
    out_specs = (P(("wide", "narrow"), None), P(), P())
    return jax.shard_map(
        per_device, mesh=mesh, in_specs=in_specs, out_specs=out_specs, check_vma=False
    )
```

```python
import jax
import jax.numpy as jnp
from jax import lax
from jax.experimental import pallas as pl
from jax.experimental.pallas import tpu as pltpu
from jax.sharding import PartitionSpec as P

MESH = pl.DeviceIdType.MESH


def position():
    w = lax.axis_index("wide")
    n = lax.axis_index("narrow")
    return w // 8, (w // 2) % 4, (w % 2) * 4 + n // 2, n % 2


def device(y, x, z, c):
    return ((y * 4 + x) * 2 + z // 4, (z % 4) * 2 + c)


CHUNKS = 4
ROWS = 128 // CHUNKS
WIDTH = 896
Z, OY, OX, PX, PY, CTX, PAIR, UP, DOWN = range(9)
SLOTS = 256
ORDER = (
    (OY, 1, 0), (OY, 1, 1), (OX, 0, 1, 0), (OX, 0, 1, 1), (CTX, 0, 0, 0), (CTX, 1, 0, 0), (OY, 2, 0), (OX, -1, 1, 0),
    (OX, -1, 1, 1), (OY, 2, 1), (Z,), (OX, 1, 1, 0), (OX, 1, 1, 1), (CTX, 0, 1, 0), (CTX, 1, 1, 0), (OX, 0, 2, 0),
    (OX, 0, 2, 1), (OY, 3, 0), (OY, 3, 1), (OX, -2, 1, 0), (OX, -2, 1, 1), (PY, 0, 1, 0), (PY, 0, 1, 1),
    (OX, -1, 2, 0), (OX, -1, 2, 1), (CTX, 0, 0, 1), (CTX, 1, 0, 1), (OY, 4, 0), (OY, 4, 1), (OX, 2, 1, 0),
    (OX, 2, 1, 1), (PY, 0, 2, 0), (PY, 0, 2, 1), (PX, 1, 0), (PX, 1, 1), (CTX, 0, 2, 0), (CTX, 1, 2, 0),
    (OX, 1, 2, 0), (OX, 1, 2, 1), (PY, 0, 3, 0), (PY, 0, 3, 1), (OX, -3, 1, 0), (OX, -3, 1, 1), (CTX, 0, 1, 1),
    (CTX, 1, 1, 1), (PY, -1, 1, 0), (PY, -1, 1, 1), (OX, 3, 1, 0), (OX, 3, 1, 1), (OX, -2, 2, 0), (OX, -2, 2, 1),
    (PY, 1, 1, 0), (PY, 1, 1, 1), (PY, 0, 4, 0), (PY, 0, 4, 1), (OX, 4, 1, 0), (OX, 4, 1, 1), (CTX, 0, 3, 0),
    (CTX, 1, 3, 0), (OX, 2, 2, 0), (OX, 2, 2, 1), (PY, -1, 2, 0), (PY, -1, 2, 1), (PX, 2, 0), (PX, 2, 1),
    (OX, -3, 2, 0), (OX, -3, 2, 1), (PY, 1, 2, 0), (PY, 1, 2, 1), (OX, 3, 2, 0), (OX, 3, 2, 1), (CTX, 0, 0, 2),
    (CTX, 1, 0, 2), (OX, 4, 2, 0), (OX, 4, 2, 1), (PY, -1, 3, 0), (PY, -1, 3, 1), (PY, 2, 1, 0), (PY, 2, 1, 1),
    (CTX, 0, 2, 1), (CTX, 1, 2, 1), (PY, 1, 3, 0), (PY, 1, 3, 1), (PY, -1, 4, 0), (PY, -1, 4, 1), (CTX, 0, 1, 2),
    (CTX, 1, 1, 2), (PY, 2, 2, 0), (PY, 2, 2, 1), (PY, 1, 4, 0), (PY, 1, 4, 1), (CTX, 0, 3, 1), (CTX, 1, 3, 1),
    (PY, 2, 3, 0), (PY, 2, 3, 1), (PY, 2, 4, 0), (PY, 2, 4, 1), (CTX, 0, 2, 2), (CTX, 1, 2, 2), (CTX, 0, 3, 2),
    (CTX, 1, 3, 2),
)


def fused_kernel(ctx_ref, pack_ref, res_ref, o_ref, wbuf, cbuf, down, acc, part, pair, line, up_in, down_in, local, send_sems, recv_sems):
    y, x, z, c = position()
    j = z % 4
    n = j * 2 + c
    zh = z // 4
    sibling = device(y, x, z, 1 - c)
    y_dev = (device((y + 1) % 8, x, z, c), device((y + 7) % 8, x, z, c))
    x_dev = (device(y, (x + 1) % 4, z, c), device(y, (x + 3) % 4, z, c))
    z_dev = (device(y, x, (z + 1) % 8, c), device(y, x, (z + 7) % 8, c))
    z_far = device(y, x, (z + 4) % 8, c)

    barrier = pltpu.get_barrier_semaphore()
    partners = [sibling, *y_dev, *x_dev, *z_dev, z_far]
    for partner in partners:
        pl.semaphore_signal(barrier, inc=1, device_id=partner, device_id_type=MESH)
    pl.semaphore_wait(barrier, len(partners))

    slots = {}
    sent = []

    def slot(key):
        return slots.setdefault(key, len(slots))

    def remote(key, src, dst, to):
        at = slot(key)
        return pltpu.make_async_remote_copy(
            src_ref=src, dst_ref=dst, send_sem=send_sems.at[at], recv_sem=recv_sems.at[at], device_id=to, device_id_type=MESH
        )

    def only(chips, action):
        if chips is None:
            action()
            return
        for chip in chips:
            pl.when(j == chip)(action)

    def send(key, make, chips=None):
        only(chips, lambda: remote(key, *make()).start())
        sent.append((key, make, chips))

    def wait(key, region):
        remote(key, region, region, sibling).wait_recv()

    def block(first, dy, dx, part_of=None):
        side = zh if first else 1 - zh
        at = (((y + dy + 8) % 8) * 4 + (x + dx + 4) % 4) * 2 + side
        if part_of is None:
            return wbuf.at[at]
        return wbuf.at[at, pl.ds(32 * part_of, 32)]

    def same(region, to):
        return lambda: (region(), region(), to)

    def lanes(t, index):
        return cbuf.at[:, pl.ds(t * ROWS, ROWS), pl.ds(pl.multiple_of(index * 384, 128), 384)]

    def mine(t):
        return ctx_ref.at[:, pl.ds(t * ROWS, ROWS), :]

    def start_ox(dy):
        for s in (0, 1):
            if dy == 0:
                send((OX, 0, 1, s), lambda s=s: (pack_ref, block(True, 0, 0), x_dev[s]))
            else:
                send((OX, dy, 1, s), same(lambda: block(True, dy, 0), x_dev[s]))

    def start_py(q):
        for s in (0, 1):
            send((PY, q, 1, s), same(lambda: block(False, 0, q), y_dev[s]))

    def own_ctx(t, side, chips):
        if chips:
            send((CTX, side, t, 0), lambda: (mine(t), lanes(t, n), z_dev[side]), chips)

    seen = set()

    def both(key):
        seen.add(key)
        return key[:-1] + (1 - key[-1],) in seen

    def event(key):
        kind = key[0]
        side = key[-1]
        if kind == Z:
            wait(key, block(False, 0, 0))
            for s in (0, 1):
                send((PX, 1, s), same(lambda: block(False, 0, 0), x_dev[s]))
            start_py(0)
        elif kind == OY:
            s = key[1]
            sign = -1 if side == 0 else 1
            half = None if s < 4 else side
            wait(key, block(True, sign * s, 0, half))
            if s < 4:
                nxt = None if s < 3 else side
                send((OY, s + 1, side), same(lambda: block(True, sign * s, 0, nxt), y_dev[side]))
                start_ox(sign * s)
            elif both(key):
                start_ox(4)
        elif kind == OX:
            dy, s = key[1], key[2]
            sign = -1 if side == 0 else 1
            wait(key, block(True, dy, sign * s, None if s == 1 else side))
            if s == 1:
                send((OX, dy, 2, side), same(lambda: block(True, dy, sign, side), x_dev[side]))
        elif kind == PX:
            s = key[1]
            sign = -1 if side == 0 else 1
            wait(key, block(False, 0, sign * s, None if s == 1 else side))
            if s == 1:
                send((PX, 2, side), same(lambda: block(False, 0, sign, side), x_dev[side]))
                start_py(sign)
            elif both(key):
                start_py(2)
        elif kind == PY:
            q, s = key[1], key[2]
            sign = -1 if side == 0 else 1
            wait(key, block(False, sign * s, q, None if s < 4 else side))
            if s < 4:
                nxt = None if s < 3 else side
                send((PY, q, s + 1, side), same(lambda: block(False, sign * s, q, nxt), y_dev[side]))
        else:
            _, side, t, h = key
            sign = -1 if side == 0 else 1
            chips = range(1 + h, 4) if side == 0 else range(0, 3 - h)
            region = lambda: lanes(t, (j + sign * (1 + h)) * 2 + c)
            only(chips, lambda: wait(key, region()))
            onward = [k for k in chips if (k < 3 if side == 0 else k > 0)]
            if onward:
                send((CTX, side, t, h + 1), same(region, z_dev[side]), onward)
            send((CTX, side + 2, t, h), same(region, sibling), chips)
            if h == 0 and t + 2 < CHUNKS:
                own_ctx(t + 2, side, (1, 2))

    send((Z,), lambda: (pack_ref, block(True, 0, 0), z_far))
    for s in (0, 1):
        send((OY, 1, s), lambda s=s: (pack_ref, block(True, 0, 0), y_dev[s]))
    start_ox(0)
    for t in range(CHUNKS):
        if t < 2:
            own_ctx(t, 0, (0, 1, 2))
            own_ctx(t, 1, (1, 2, 3))
        else:
            own_ctx(t, 0, (0,))
            own_ctx(t, 1, (3,))
    for t in range(CHUNKS):
        send((CTX, 4, t, 0), lambda t=t: (mine(t), lanes(t, n), sibling))
    keep_w = pltpu.make_async_copy(pack_ref, block(True, 0, 0), local.at[0])
    keep_w.start()
    every = pl.ds(pl.multiple_of(n * 384, 128), 384)
    keep_c = pltpu.make_async_copy(ctx_ref, cbuf.at[:, :, every], local.at[1])
    keep_c.start()

    for key in ORDER:
        event(key)
    keep_w.wait()
    keep_c.wait()

    lane = lax.broadcasted_iota(jnp.int32, (128, 1024), 1)
    step = lax.broadcasted_iota(jnp.int32, (128, 1024), 0)

    def pick_rows(s, carry):
        want = (lane >> 4) * 12 + (lane & 15)
        pick = jnp.where(((lane & 15) < 12) & (want == step + s * 128), 1.0, 0.0).astype(jnp.bfloat16)
        picked = jnp.dot(pick, wbuf[:, 48:64, :].reshape(1024, 768), preferred_element_type=jnp.float32)
        down[pl.ds(pl.multiple_of(s * 128, 128), 128), :] = picked.astype(jnp.bfloat16)
        return carry

    lax.fori_loop(0, 6, pick_rows, 0)

    gain = pack_ref[60:61, :].astype(jnp.float32)

    def compute(t):
        here = pl.ds(t * ROWS, ROWS)
        for h in range(3):
            for side in (0, 1):
                chips = range(1 + h, 4) if side == 0 else range(0, 3 - h)
                sign = -1 if side == 0 else 1
                only(chips, lambda: wait((CTX, side + 2, t, h), lanes(t, (j + sign * (1 + h)) * 2 + 1 - c)))
        wait((CTX, 4, t, 0), lanes(t, j * 2 + 1 - c))
        acc[...] = jnp.zeros_like(acc)

        def accumulate(k, carry):
            lhs = cbuf[:, here, pl.ds(pl.multiple_of(k * 384, 128), 384)].reshape(8 * ROWS, 384)
            rhs = wbuf[pl.ds(pl.multiple_of(k * 8, 8), 8), 0:48, :].reshape(384, 768)
            acc[...] += jnp.dot(lhs, rhs, preferred_element_type=jnp.float32)
            return carry

        lax.fori_loop(0, 8, accumulate, 0)
        stream = (res_ref[:, here, :].reshape(8 * ROWS, 768).astype(jnp.float32) + acc[...]).astype(jnp.bfloat16)
        value = stream.astype(jnp.float32)
        total = jnp.sum(value, axis=1, keepdims=True)
        squares = jnp.sum(value * value, axis=1, keepdims=True)
        scaled = (value * gain).astype(jnp.bfloat16)
        mapped = lax.dot_general(scaled, down[...], (((1,), (1,)), ((), ())), preferred_element_type=jnp.float32)
        column = lax.broadcasted_iota(jnp.int32, (8 * ROWS, 128), 1)
        stats = jnp.where(column == 0, total, jnp.where(column == 1, squares, 0.0))
        for k in range(8):
            cut = slice(k * ROWS, (k + 1) * ROWS)
            part[t, k % 2, k // 2, 0:ROWS, 0:768] = mapped[cut]
            part[t, k % 2, k // 2, 0:ROWS, 768:896] = stats[cut]
        if t == 0:
            rows = jnp.broadcast_to(gain, (16, 768)).astype(jnp.bfloat16)
            gain_rows = lax.dot_general(rows, down[...], (((1,), (1,)), ((), ())), preferred_element_type=jnp.float32)
            for k in range(8):
                part[0, k % 2, k // 2, ROWS:ROWS + 8, 0:768] = gain_rows[0:8]
                part[0, k % 2, k // 2, ROWS:ROWS + 8, 768:896] = jnp.zeros((8, 128), jnp.float32)

    def tall(t):
        return ROWS + 8 if t == 0 else ROWS

    def piece(ref, t, dest):
        return ref.at[t, dest, pl.ds(0, tall(t))]

    def pair_up(t):
        rows = pl.ds(0, tall(t))
        send((PAIR, t), lambda: (part.at[t, 1 - c, :, rows], pair.at[t, :, rows], sibling))

    def add_pair(t):
        rows = pl.ds(0, tall(t))
        wait((PAIR, t), pair.at[t, :, rows])
        line[t, :, rows] = part[t, c, :, rows] + pair[t, :, rows]
        pass_on(t, 0, 0)
        pass_on(t, 3, 1)

    def pass_on(t, chip, side):
        kind, arrived = ((UP, up_in), (DOWN, down_in))[side]
        first = chip == (0 if side == 0 else 3)
        for dest in (range(3, chip, -1) if side == 0 else range(chip)):
            if not first:

                def add():
                    wait((kind, t, dest), piece(arrived, t, dest))
                    line[t, dest, 0:tall(t)] += arrived[t, dest, 0:tall(t)]

                only((chip,), add)
            send((kind, t, dest), lambda dest=dest: (piece(line, t, dest), piece(arrived, t, dest), z_dev[side]), (chip,))

    def finish(t):
        for chip in range(4):

            def add():
                total = line[t, chip, 0:tall(t)]
                if chip > 0:
                    wait((UP, t, chip), piece(up_in, t, chip))
                    total = total + up_in[t, chip, 0:tall(t)]
                if chip < 3:
                    wait((DOWN, t, chip), piece(down_in, t, chip))
                    total = total + down_in[t, chip, 0:tall(t)]
                o_ref[t * ROWS:(t + 1) * ROWS, :] = total[0:ROWS]
                if t == 0:
                    o_ref[128:136, :] = total[ROWS:ROWS + 8]

            only((chip,), add)

    stages = (
        lambda t: (compute(t), pair_up(t)),
        add_pair,
        lambda t: (pass_on(t, 1, 0), pass_on(t, 2, 1)),
        lambda t: (pass_on(t, 2, 0), pass_on(t, 1, 1)),
        finish,
    )
    for beat in range(CHUNKS + len(stages) - 1):
        for depth, stage in enumerate(stages):
            if 0 <= beat - depth < CHUNKS:
                stage(beat - depth)
    for key, make, chips in sent:
        only(chips, lambda: remote(key, *make()).wait_send())


def fused(context, pack, residual):
    vmem = pl.BlockSpec(memory_space=pltpu.VMEM)
    tall = ROWS + 8
    f32 = jnp.float32
    bf16 = jnp.bfloat16
    return pl.pallas_call(
        fused_kernel,
        out_shape=jax.ShapeDtypeStruct((136, WIDTH), f32),
        in_specs=[vmem] * 3,
        out_specs=vmem,
        scratch_shapes=[
            pltpu.VMEM((64, 64, 768), bf16),
            pltpu.VMEM((8, 128, 3072), bf16),
            pltpu.VMEM((768, 768), bf16),
            pltpu.VMEM((8 * ROWS, 768), f32),
            pltpu.VMEM((CHUNKS, 2, 4, tall, WIDTH), f32),
            pltpu.VMEM((CHUNKS, 4, tall, WIDTH), f32),
            pltpu.VMEM((CHUNKS, 4, tall, WIDTH), f32),
            pltpu.VMEM((CHUNKS, 4, tall, WIDTH), f32),
            pltpu.VMEM((CHUNKS, 4, tall, WIDTH), f32),
            pltpu.SemaphoreType.DMA((2,)),
            pltpu.SemaphoreType.DMA((SLOTS,)),
            pltpu.SemaphoreType.DMA((SLOTS,)),
        ],
        compiler_params=pltpu.CompilerParams(collective_id=0, has_side_effects=True, vmem_limit_bytes=60000 * 1024),
        name="gather_map",
    )(context.reshape(8, 128, 384), pack, residual.reshape(8, 128, 768))


def ar_kernel(f_ref, g_ref, f_out, g_out, buf0, half, buf_a, mid, buf_b, buf_x, tail, fin, sems_s, sems_r):
    y, x, z, c = position()
    on_z = 1 - c
    pos_a = z * on_z + y * c
    pos_b = y * on_z + z * c

    def along_a(d):
        return device((y + d * c) % 8, x, (z + d * on_z) % 8, c)

    def along_b(d):
        return device((y + d * on_z) % 8, x, (z + d * c) % 8, c)

    def along_x(d):
        return device(y, (x + d) % 4, z, c)

    sibling = device(y, x, z, 1 - c)
    barrier = pltpu.get_barrier_semaphore()
    partners = [sibling] + [along_a(d) for d in range(1, 8)] + [along_b(d) for d in range(1, 8)] + [along_x(d) for d in range(1, 4)]
    for partner in partners:
        pl.semaphore_signal(barrier, inc=1, device_id=partner, device_id_type=MESH)
    pl.semaphore_wait(barrier, len(partners))
    sent = []

    def send(src, dst, slot, to):
        copy = pltpu.make_async_remote_copy(
            src_ref=src, dst_ref=dst, send_sem=sems_s.at[slot], recv_sem=sems_r.at[slot], device_id=to, device_id_type=MESH
        )
        copy.start()
        sent.append(copy)
        return copy

    def own(total, mine):
        copy = pltpu.make_async_remote_copy(
            src_ref=mine, dst_ref=buf0, send_sem=sems_s.at[0], recv_sem=sems_r.at[0], device_id=sibling, device_id_type=MESH
        )
        copy.start()
        copy.wait()
        half[...] = total[...] + buf0[...]

    @pl.when(c == 0)
    def _():
        own(f_ref, g_ref)

    @pl.when(c == 1)
    def _():
        own(g_ref, f_ref)

    def rows(ref, at, n):
        return ref.at[pl.ds(pl.multiple_of(at * n, 8), n)]

    copies = [
        send(rows(half, (pos_a + d) % 8, 48), buf_a.at[d - 1], d, along_a(d)) for d in range(1, 8)
    ]
    total = half[pl.ds(pl.multiple_of(pos_a * 48, 8), 48), :]
    for d in range(1, 8):
        copies[d - 1].wait_recv()
        total = total + buf_a[d - 1]
    mid[0:48, :] = total
    mid[48:64, :] = jnp.zeros((16, 384), jnp.float32)
    copies = [
        send(rows(mid, (pos_b + d) % 8, 8), buf_b.at[d - 1], 7 + d, along_b(d)) for d in range(1, 8)
    ]
    total = mid[pl.ds(pl.multiple_of(pos_b * 8, 8), 8), :]
    for d in range(1, 8):
        copies[d - 1].wait_recv()
        total = total + buf_b[d - 1]
    buf_x[x] = total
    copies = [send(buf_x.at[x], buf_x.at[x], 14 + d, along_x(d)) for d in range(1, 4)]
    for copy in copies:
        copy.wait_recv()
    tail[pl.ds(pl.multiple_of(pos_b * 8, 8), 8), :] = (buf_x[0] + buf_x[1]) + (buf_x[2] + buf_x[3])
    copies = [send(rows(tail, pos_b, 8), rows(tail, pos_b, 8), 17 + d, along_b(d)) for d in range(1, 8)]
    for copy in copies:
        copy.wait_recv()
    place = pl.ds(pl.multiple_of(pos_a * 48, 8), 48)
    copies = [send(tail.at[pl.ds(0, 48)], fin.at[c, place], 24 + d, along_a(d)) for d in range(1, 8)]
    shares = [send(tail.at[pl.ds(0, 48)], fin.at[c, place], 32, sibling)]
    fin[c, place, :] = tail[0:48, :]
    for d in range(1, 8):
        copies[d - 1].wait_recv()
        there = pl.ds(pl.multiple_of((pos_a + 8 - d) % 8 * 48, 8), 48)
        shares.append(send(fin.at[c, there], fin.at[c, there], 32 + d, sibling))
    for copy in shares:
        copy.wait_recv()
    f_out[...] = fin[0]
    g_out[...] = fin[1]
    for copy in sent:
        copy.wait_send()


def all_reduce(f_local, g_local):
    size = f_local.shape[0]
    vmem = pl.BlockSpec(memory_space=pltpu.VMEM)
    full = jax.ShapeDtypeStruct((size, size), jnp.float32)
    return pl.pallas_call(
        ar_kernel,
        out_shape=(full, full),
        in_specs=[vmem, vmem],
        out_specs=(vmem, vmem),
        scratch_shapes=[
            pltpu.VMEM((size, size), jnp.float32),
            pltpu.VMEM((size, size), jnp.float32),
            pltpu.VMEM((7, size // 8, size), jnp.float32),
            pltpu.VMEM((64, size), jnp.float32),
            pltpu.VMEM((7, 8, size), jnp.float32),
            pltpu.VMEM((4, 8, size), jnp.float32),
            pltpu.VMEM((64, size), jnp.float32),
            pltpu.VMEM((2, size, size), jnp.float32),
            pltpu.SemaphoreType.DMA((40,)),
            pltpu.SemaphoreType.DMA((40,)),
        ],
        compiler_params=pltpu.CompilerParams(collective_id=1, has_side_effects=True),
        name="gradient_sum",
    )(f_local, g_local)


def coupling(values, weight):
    return jax.nn.gelu(jnp.dot(values, weight, precision=lax.Precision.HIGHEST))


def per_device(context, out_weight, residual, ln_gain, side_down, f_weight, g_weight, targets):
    blank = jnp.zeros((3, ln_gain.shape[0]), jnp.bfloat16)
    pack = jnp.concatenate([out_weight, side_down.T, ln_gain[None, :], blank], axis=0)
    sums = fused(context, pack, residual)
    local_rows = targets.shape[0]
    side = side_down.shape[1] * lax.axis_size("wide")
    projected = sums[:local_rows, :side]
    token_sum = sums[:local_rows, side]
    token_squares = sums[:local_rows, side + 1]
    gain_map = sums[local_rows, :side]
    features = residual.shape[1] * lax.axis_size("narrow")
    mean = token_sum / features
    spread = token_squares / features - mean * mean
    side_in = (projected - mean[:, None] * gain_map[None, :]) / jnp.sqrt(spread + 1e-06)[:, None]
    half = side_in.shape[1] // 2
    f_w = f_weight.astype(jnp.float32)
    g_w = g_weight.astype(jnp.float32)
    first = side_in[:, :half]
    second = side_in[:, half:]
    upper = first + coupling(second, f_w)
    g_value, g_pull = jax.vjp(coupling, upper, g_w)
    lower = second + g_value
    side_out = jnp.concatenate([upper, lower], axis=1)
    all_tokens = local_rows * lax.axis_size("wide") * lax.axis_size("narrow")
    misfit = (side_out - targets) / all_tokens
    upper_back, g_local = g_pull(misfit[:, half:])
    rebuilt = lower - g_value
    upper_total = misfit[:, :half] + upper_back
    f_value, f_pull = jax.vjp(coupling, rebuilt, f_w)
    f_local = f_pull(upper_total)[1]
    f_total, g_total = all_reduce(f_local, g_local)
    return (side_out, f_total, g_total)


def solution(mesh):
    in_specs = (
        P("wide", "narrow"),
        P("wide", "narrow"),
        P("wide", "narrow"),
        P("narrow"),
        P("narrow", "wide"),
        P(),
        P(),
        P(("wide", "narrow"), None),
    )
    out_specs = (P(("wide", "narrow"), None), P(), P())
    return jax.shard_map(
        per_device, mesh=mesh, in_specs=in_specs, out_specs=out_specs, check_vma=False
    )
```

```python
import math

import jax
import jax.numpy as jnp
from jax import lax
from jax.experimental import pallas as pl
from jax.experimental.pallas import tpu as pltpu
from jax.sharding import PartitionSpec as P

MESH = pl.DeviceIdType.MESH


def position():
    w = lax.axis_index("wide")
    n = lax.axis_index("narrow")
    return w // 8, (w // 2) % 4, (w % 2) * 4 + n // 2, n % 2


def device(y, x, z, c):
    return ((y * 4 + x) * 2 + z // 4, (z % 4) * 2 + c)


CHUNKS = 4
ROWS = 128 // CHUNKS
WIDTH = 896
SLOTS = 320
LEAD = 2
Z, O, PW, PD, CTX, PICK, UNIT, PROJ, PAIR, P1, P2, FIN, UP, DOWN, GRAD = range(15)
FAR_FIRST = (4, 3, 5, 2, 6, 1, 7)
NEAR_FIRST = (1, 7, 2, 6, 3, 5, 4)
TOKENS = 65536
PLANES = ((0, 1), (-1, 2), (-2, 3), (-3, 4))
SPAN = {O: (0, 64), PW: (0, 48), PD: (48, 16)}
ORDER = (
    (O, 0, 0, 1, 0), (O, 0, 0, 1, 1), (O, 1, 0, 1, 0), (O, 1, 0, 1, 1), (CTX, 0, 0, 0), (CTX, 1, 0, 0),
    (O, 0, 0, 2, 0), (O, 0, 0, 2, 1), (O, 1, 0, 2, 0), (Z,), (O, 1, 0, 2, 1), (O, 0, -1, 1, 0), (O, 0, -1, 1, 1),
    (CTX, 0, 1, 0), (CTX, 1, 1, 0), (O, 0, 1, 1, 0), (O, 0, 1, 1, 1), (PW, 1, 0, 1, 1), (O, 1, 0, 3, 0),
    (PD, 1, 0, 1, 1), (O, 0, -2, 1, 0), (O, 0, -2, 1, 1), (PW, 1, 0, 1, 0), (PD, 1, 0, 1, 0), (O, 1, 0, 3, 1),
    (CTX, 0, 0, 1), (CTX, 1, 0, 1), (PW, 0, 0, 1, 0), (PW, 0, 0, 1, 1), (PD, 0, 0, 1, 0), (O, 1, 0, 4, 0),
    (PD, 0, 0, 1, 1), (PW, 1, 0, 2, 1), (PD, 1, 0, 2, 1), (PW, 1, 0, 2, 0), (O, 0, 2, 1, 0), (O, 0, 2, 1, 1),
    (O, 1, 0, 4, 1), (PD, 1, 0, 2, 0), (O, 0, -1, 2, 0), (O, 0, -1, 2, 1), (CTX, 0, 2, 0), (CTX, 1, 2, 0),
    (PW, 1, -1, 1, 1), (PW, 1, -1, 1, 0), (O, 0, 1, 2, 0), (O, 0, 1, 2, 1), (PW, 1, 1, 1, 1), (PW, 1, 1, 1, 0),
    (O, 0, -3, 1, 0), (O, 0, -3, 1, 1), (PD, 0, 1, 1, 0), (PD, 0, 1, 1, 1), (PW, 1, 0, 3, 1), (PW, 1, 0, 3, 0),
    (PD, 1, 0, 3, 1), (CTX, 0, 1, 1), (CTX, 1, 1, 1), (PD, 1, 0, 3, 0), (O, 0, -2, 2, 0), (O, 0, -2, 2, 1),
    (PD, 0, -1, 1, 0), (PD, 0, -1, 1, 1), (PW, 1, -1, 2, 1), (PW, 1, -1, 2, 0), (O, 0, 3, 1, 0), (O, 0, 3, 1, 1),
    (PW, 1, 1, 2, 1), (PW, 1, 1, 2, 0), (PW, 0, 0, 2, 1), (PW, 1, 0, 4, 1), (PW, 0, 0, 2, 0), (PD, 0, 2, 1, 1),
    (CTX, 0, 3, 0), (CTX, 1, 3, 0), (PW, 1, 0, 4, 0), (PD, 0, 0, 2, 0), (PD, 1, 0, 4, 0), (PD, 0, 2, 1, 0),
    (O, 0, 2, 2, 1), (PW, 1, -1, 3, 1), (PICK, 0), (O, 0, 2, 2, 0), (PW, 1, -1, 3, 0), (PW, 1, 1, 3, 1),
    (O, 0, 4, 1, 1), (PD, 0, -2, 1, 1), (PW, 1, 1, 3, 0), (O, 0, 4, 1, 0), (PW, 1, 2, 1, 1), (CTX, 0, 0, 2),
    (CTX, 1, 0, 2), (PD, 0, -2, 1, 0), (O, 0, -3, 2, 1), (PD, 0, 1, 2, 1), (PW, 1, -1, 4, 1), (PW, 1, 2, 1, 0),
    (O, 0, -3, 2, 0), (PD, 0, 3, 1, 1), (PW, 1, -1, 4, 0), (PD, 0, 3, 1, 0), (PD, 0, -3, 1, 1), (PW, 1, 1, 4, 1),
    (PW, 1, 1, 4, 0), (PD, 0, -3, 1, 0), (PD, 0, -1, 2, 1), (PICK, 1), (PICK, -1), (UNIT, 0, 0), (O, 0, 3, 2, 0),
    (O, 0, 3, 2, 1), (PW, 1, 2, 2, 1), (PD, 0, 4, 1, 0), (PD, 0, 4, 1, 1), (CTX, 0, 2, 1), (CTX, 1, 2, 1),
    (PD, 0, 2, 2, 0), (PW, 1, 2, 2, 0), (PICK, 2), (UNIT, 1, 0), (O, 0, 4, 2, 1), (O, 0, 4, 2, 0), (PD, 0, 3, 2, 1),
    (PD, 0, -2, 2, 0), (PD, 0, -3, 2, 1), (PICK, 3), (PD, 0, 4, 2, 0), (PICK, -2), (PICK, -3), (PICK, 4),
    (PW, 1, 2, 3, 1), (UNIT, 2, 0), (PW, 1, 2, 3, 0), (CTX, 0, 1, 2), (CTX, 1, 1, 2), (PW, 1, 2, 4, 1), (UNIT, 0, 1),
    (PW, 1, 2, 4, 0), (UNIT, 3, 0), (PROJ, 0), (CTX, 0, 3, 1), (CTX, 1, 3, 1), (UNIT, 1, 1), (UNIT, 2, 1),
    (UNIT, 3, 1), (PAIR, 0), (PROJ, 1), (CTX, 0, 2, 2), (CTX, 1, 2, 2), (PAIR, 1), (P1, 0, 0), (UNIT, 0, 2),
    (CTX, 0, 3, 2), (CTX, 1, 3, 2), (UNIT, 1, 2), (UNIT, 2, 2), (P1, 0, 1), (UNIT, 3, 2), (PROJ, 2), (P2, 0),
    (UNIT, 0, 3), (UNIT, 1, 3), (UNIT, 2, 3), (UNIT, 3, 3), (PAIR, 2), (P1, 1, 0), (PROJ, 3), (FIN, 0), (P1, 1, 1),
    (PAIR, 3), (P2, 1), (P1, 2, 0), (P1, 2, 1), (FIN, 1), (P2, 2), (P1, 3, 0), (FIN, 2), (P1, 3, 1), (P2, 3),
    (FIN, 3),
)


def half(kind, side, flip):
    if kind == O:
        return (32 * side, 32)
    if kind == PW:
        return ((0, 32), (32, 16))[side] if flip == 0 else ((0, 16), (16, 32))[side]
    return (48, 16) if side == flip else None


def split(value):
    high = value.astype(jnp.bfloat16)
    rest = value - high.astype(jnp.float32)
    middle = rest.astype(jnp.bfloat16)
    low = (rest - middle.astype(jnp.float32)).astype(jnp.bfloat16)
    return high, middle, low


def exact_dot(value, weight, contract):
    rows = value.shape[0]
    tall = lax.dot_general(
        jnp.concatenate(split(value), axis=0), weight, (((1,), (contract,)), ((), ())), preferred_element_type=jnp.float32
    )
    return (tall[2 * rows:] + tall[rows:2 * rows]) + tall[:rows]


def gelu_and_slope(v):
    scale = math.sqrt(2.0 / math.pi)
    square = v * v
    bent = jnp.tanh(scale * (v + 0.044715 * (square * v)))
    share = 0.5 * (1.0 + bent)
    slope = share + 0.5 * v * (1.0 - bent * bent) * (scale * (1.0 + 3.0 * 0.044715 * square))
    return v * share, slope


def fused_kernel(
    ctx_ref, weight_ref, side_ref, gain_ref, res_hbm, f_hbm, g_hbm, targets_hbm, o_ref, f_out, g_out,
    pack_ref, res_ref, f_ref, g_ref, targets_ref, wbuf, cbuf, down, acc, part, pair, line, up_in, down_in, sums,
    grads, buf0, summed, buf_a, mid, buf_b, buf_x, tail, fin, local, send_sems, recv_sems
):
    y, x, z, c = position()
    j = z % 4
    n = j * 2 + c
    zh = z // 4
    sibling = device(y, x, z, 1 - c)
    y_dev = (device((y + 1) % 8, x, z, c), device((y + 7) % 8, x, z, c))
    x_dev = (device(y, (x + 1) % 4, z, c), device(y, (x + 3) % 4, z, c))
    z_dev = (device(y, x, (z + 1) % 8, c), device(y, x, (z + 7) % 8, c))
    z_far = device(y, x, (z + 4) % 8, c)

    on_z = 1 - c
    pos_a = z * on_z + y * c
    pos_b = y * on_z + z * c

    def along_a(d):
        return device((y + d * c) % 8, x, (z + d * on_z) % 8, c)

    def along_b(d):
        return device((y + d * on_z) % 8, x, (z + d * c) % 8, c)

    def along_x(d):
        return device(y, (x + d) % 4, z, c)

    barrier = pltpu.get_barrier_semaphore()
    partners = [sibling]
    partners += [along_a(d) for d in range(1, 8)] + [along_b(d) for d in range(1, 8)] + [along_x(d) for d in range(1, 4)]
    for partner in partners:
        pl.semaphore_signal(barrier, inc=1, device_id=partner, device_id_type=MESH)
    loads = [
        pltpu.make_async_copy(src, dst, local.at[2 + i])
        for i, (src, dst) in enumerate(
            ((res_hbm, res_ref), (f_hbm, f_ref), (g_hbm, g_ref), (targets_hbm, targets_ref))
        )
    ]
    for load in loads:
        load.start()
    pack_ref[0:48, :] = weight_ref[...]
    pack_ref[48:64, :] = jnp.zeros((16, 768), jnp.bfloat16)
    pack_ref[48:60, :] = side_ref[...]
    pl.semaphore_wait(barrier, len(partners))

    slots = {}
    sent = []
    begun = set()

    def remote(key, src, dst, to):
        at = slots.setdefault(key, len(slots))
        return pltpu.make_async_remote_copy(
            src_ref=src, dst_ref=dst, send_sem=send_sems.at[at], recv_sem=recv_sems.at[at], device_id=to, device_id_type=MESH
        )

    def only(chips, action):
        if chips is None:
            action()
            return
        for chip in chips:
            pl.when(j == chip)(action)

    def send(key, make, chips=None):
        only(chips, lambda: remote(key, *make()).start())
        sent.append((key, make, chips))

    def wait(key, region):
        remote(key, region, region, sibling).wait_recv()

    def plane(dy):
        return (y + dy + 8) % 8

    def block(kind, dy, dx, span=None):
        start, count = span or SPAN[kind]
        side = zh if kind == O else 1 - zh
        at = (plane(dy) * 4 + (x + dx + 4) % 4) * 2 + side
        return wbuf.at[at, pl.ds(start, count)]

    def send_block(key, kind, dy, dx, to, span=None):
        if kind == O and dy == 0 and dx == 0:
            send(key, lambda: (pack_ref, block(O, 0, 0), to))
        else:
            send(key, lambda: (block(kind, dy, dx, span), block(kind, dy, dx, span), to))

    def start_x(kind, dy):
        for s in (0, 1):
            send_block((kind, 0, dy, 1, s), kind, dy, 0, x_dev[s])

    def start_y(q):
        for s in (0, 1):
            send_block((PW, 1, q, 1, s), PW, 0, q, y_dev[s])

    def lanes(t, index):
        return cbuf.at[:, pl.ds(t * ROWS, ROWS), pl.ds(pl.multiple_of(index * 384, 128), 384)]

    def mine(t):
        return ctx_ref.at[:, pl.ds(t * ROWS, ROWS), :]

    def own_ctx(t, side, chips):
        send((CTX, side, t, 0), lambda: (mine(t), lanes(t, n), z_dev[side]), chips)

    def after_both(key):
        twin = key[:-1] + (1 - key[-1],)
        begun.add(key)
        return twin in begun

    def z_event(key):
        wait(key, wbuf.at[(y * 4 + x) * 2 + 1 - zh])
        for s in (0, 1):
            send_block((PW, 0, 0, 1, s), PW, 0, 0, x_dev[s])
        start_y(0)
        for s in (0, 1):
            send_block((PD, 1, 0, 1, s), PD, 0, 0, y_dev[s])
        start_x(PD, 0)

    def y_first(key):
        kind, _, _, s, side = key
        dy = (-1 if side == 0 else 1) * s
        wait(key, block(kind, dy, 0, half(kind, side, 0) if s == 4 else None))
        if s < 4:
            span = half(kind, side, 0) if s == 3 else SPAN[kind]
            if span:
                send_block((kind, 1, 0, s + 1, side), kind, dy, 0, y_dev[side], span)
            start_x(kind, dy)
        elif kind == PD or after_both(key):
            start_x(kind, 4)

    def x_second(key):
        kind, _, dy, s, side = key
        dx = (-1 if side == 0 else 1) * s
        span = half(kind, side, dy % 2)
        wait(key, block(kind, dy, dx, span if s == 2 else None))
        if s == 1 and span:
            send_block((kind, 0, dy, 2, side), kind, dy, dx, x_dev[side], span)

    def x_first(key):
        _, _, _, s, side = key
        dx = (-1 if side == 0 else 1) * s
        span = half(PW, side, 0)
        wait(key, block(PW, 0, dx, span if s == 2 else None))
        if s == 1:
            send_block((PW, 0, 0, 2, side), PW, 0, dx, x_dev[side], span)
            start_y(dx)
        elif after_both(key):
            start_y(2)

    def y_second(key):
        _, _, q, s, side = key
        dy = (-1 if side == 0 else 1) * s
        span = half(PW, side, q % 2)
        wait(key, block(PW, dy, q, span if s == 4 else None))
        if s < 4:
            send_block((PW, 1, q, s + 1, side), PW, dy, q, y_dev[side], span if s == 3 else None)

    def reach(side, h):
        return range(1 + h, 4) if side == 0 else range(0, 3 - h)

    def source(side, h):
        return j + (-1 if side == 0 else 1) * (1 + h)

    def ctx_event(key):
        _, side, t, h = key
        chips = reach(side, h)
        region = lambda: lanes(t, source(side, h) * 2 + c)
        onward = [k for k in chips if (k < 3 if side == 0 else k > 0)]
        only(chips, lambda: wait(key, region()))
        if onward:
            send((CTX, side, t, h + 1), lambda: (region(), region(), z_dev[side]), onward)
        send((CTX, side + 2, t, h), lambda: (region(), region(), sibling), chips)
        if h == 0 and t + LEAD < CHUNKS:
            own_ctx(t + LEAD, side, (1, 2))

    def keep():
        return pltpu.make_async_copy(pack_ref, block(O, 0, 0), local.at[0]), pltpu.make_async_copy(
            ctx_ref, cbuf.at[:, :, pl.ds(pl.multiple_of(n * 384, 128), 384)], local.at[1]
        )

    def pick(key):
        if PICK not in begun:
            begun.add(PICK)
            for copy in keep():
                copy.wait()
        lane = lax.broadcasted_iota(jnp.int32, (96, 128), 1)
        row = lax.broadcasted_iota(jnp.int32, (96, 128), 0)
        here = ((lane & 15) < 12) & ((lane >> 4) * 12 + (lane & 15) == row)
        chosen = jnp.where(here, 1.0, 0.0).astype(jnp.bfloat16)
        k = plane(key[1])
        padded = wbuf[pl.ds(pl.multiple_of(k * 8, 8), 8), 48:64, :].reshape(128, 768)
        picked = jnp.dot(chosen, padded, preferred_element_type=jnp.float32)
        down[pl.ds(pl.multiple_of(k * 96, 32), 96), :] = picked.astype(jnp.bfloat16)

    def unit(key):
        _, p, t = key
        if (CTX, t) not in begun:
            begun.add((CTX, t))
            for h in range(3):
                for side in (0, 1):
                    only(reach(side, h), lambda: wait((CTX, side + 2, t, h), lanes(t, source(side, h) * 2 + 1 - c)))
            wait((CTX, 4, t, 0), lanes(t, j * 2 + 1 - c))
        here = pl.ds(t * ROWS, ROWS)
        ks = [plane(dy) for dy in PLANES[p]]
        lhs = [cbuf[:, here, pl.ds(pl.multiple_of(k * 384, 128), 384)].reshape(8 * ROWS, 384) for k in ks]
        rhs = [wbuf[pl.ds(pl.multiple_of(k * 8, 8), 8), 0:48, :].reshape(384, 768) for k in ks]
        product = jnp.dot(
            jnp.concatenate(lhs, axis=1), jnp.concatenate(rhs, axis=0), preferred_element_type=jnp.float32
        )
        if (UNIT, t) in begun:
            acc[t] += product
        else:
            begun.add((UNIT, t))
            acc[t] = product

    def project(key):
        t = key[1]
        here = pl.ds(t * ROWS, ROWS)
        if PROJ not in begun:
            begun.add(PROJ)
            loads[0].wait()
        gain = gain_ref[...].astype(jnp.float32)
        stream = (res_ref[:, here, :].reshape(8 * ROWS, 768).astype(jnp.float32) + acc[t]).astype(jnp.bfloat16)
        value = stream.astype(jnp.float32)
        total = jnp.sum(value, axis=1, keepdims=True)
        squares = jnp.sum(value * value, axis=1, keepdims=True)
        scaled = (value * gain).astype(jnp.bfloat16)
        mapped = lax.dot_general(scaled, down[...], (((1,), (1,)), ((), ())), preferred_element_type=jnp.float32)
        column = lax.broadcasted_iota(jnp.int32, (8 * ROWS, 128), 1)
        stats = jnp.where(column == 0, total, jnp.where(column == 1, squares, 0.0))
        for k in range(8):
            cut = slice(k * ROWS, (k + 1) * ROWS)
            part[t, k % 2, k // 2, 0:ROWS, 0:768] = mapped[cut]
            part[t, k % 2, k // 2, 0:ROWS, 768:896] = stats[cut]
        if t == 0:
            rows = jnp.broadcast_to(gain, (16, 768)).astype(jnp.bfloat16)
            gain_rows = lax.dot_general(rows, down[...], (((1,), (1,)), ((), ())), preferred_element_type=jnp.float32)
            for k in range(8):
                part[0, k % 2, k // 2, ROWS:ROWS + 8, 0:768] = gain_rows[0:8]
                part[0, k % 2, k // 2, ROWS:ROWS + 8, 768:896] = jnp.zeros((8, 128), jnp.float32)
        rows_sent = pl.ds(0, tall(t))
        send((PAIR, t), lambda: (part.at[t, 1 - c, :, rows_sent], pair.at[t, :, rows_sent], sibling))

    def tall(t):
        return ROWS + 8 if t == 0 else ROWS

    def piece(ref, t, dest):
        return ref.at[t, dest, pl.ds(0, tall(t))]

    def add_pair(key):
        t = key[1]
        rows = pl.ds(0, tall(t))
        wait(key, pair.at[t, :, rows])
        line[t, :, rows] = part[t, c, :, rows] + pair[t, :, rows]
        for i in range(3):
            pass_on(t, 0, 0, 3 - i, True)
            pass_on(t, 3, 1, i, True)

    def pass_on(t, chip, side, dest, first=False):
        kind, arrived = ((UP, up_in), (DOWN, down_in))[side]
        if not first:

            def add():
                wait((kind, t, dest), piece(arrived, t, dest))
                line[t, dest, 0:tall(t)] += arrived[t, dest, 0:tall(t)]

            only((chip,), add)
        send((kind, t, dest), lambda: (piece(line, t, dest), piece(arrived, t, dest), z_dev[side]), (chip,))

    def finish(key):
        t = key[1]
        for chip in range(4):

            def add():
                total = line[t, chip, 0:tall(t)]
                if chip > 0:
                    wait((UP, t, chip), piece(up_in, t, chip))
                    total = total + up_in[t, chip, 0:tall(t)]
                if chip < 3:
                    wait((DOWN, t, chip), piece(down_in, t, chip))
                    total = total + down_in[t, chip, 0:tall(t)]
                sums[t * ROWS:(t + 1) * ROWS, :] = total[0:ROWS]
                if t == 0:
                    sums[128:136, :] = total[ROWS:ROWS + 8]

            only((chip,), add)

    def task(key):
        kind = key[0]
        if kind == Z:
            z_event(key)
        elif kind in (O, PD):
            (y_first if key[1] else x_second)(key)
        elif kind == PW:
            (y_second if key[1] else x_first)(key)
        elif kind == CTX:
            ctx_event(key)
        elif kind == P1:
            _, t, i = key
            pass_on(t, 1, 0, 3 - i)
            pass_on(t, 2, 1, i)
        elif kind == P2:
            pass_on(key[1], 2, 0, 3)
            pass_on(key[1], 1, 1, 0)
        else:
            {PICK: pick, UNIT: unit, PROJ: project, PAIR: add_pair, FIN: finish}[kind](key)

    def side_block():
        for load in loads[1:]:
            load.wait()
        mean = sums[0:128, 768:769] * (1.0 / (8 * 768))
        spread = sums[0:128, 769:770] * (1.0 / (8 * 768)) - mean * mean
        scale = 1.0 / jnp.sqrt(spread + 1e-06)
        first = (sums[0:128, 0:384] - mean * sums[128:129, 0:384]) * scale
        second = (sums[0:128, 384:768] - mean * sums[128:129, 384:768]) * scale
        bend, f_slope = gelu_and_slope(exact_dot(second, f_ref[...], 0))
        upper = first + bend
        bend, g_slope = gelu_and_slope(exact_dot(upper, g_ref[...], 0))
        lower = second + bend
        o_ref[:, 0:384] = upper
        o_ref[:, 384:768] = lower
        back = (lower - targets_ref[:, 384:768]) * (1.0 / TOKENS) * g_slope
        upper_total = (upper - targets_ref[:, 0:384]) * (1.0 / TOKENS) + exact_dot(back, g_ref[...], 1)
        whole = lax.Precision.HIGHEST
        over_tokens = (((0,), (0,)), ((), ()))
        grads[1] = lax.dot_general(upper, back, over_tokens, precision=whole, preferred_element_type=jnp.float32)
        grads[0] = lax.dot_general(second, upper_total * f_slope, over_tokens, precision=whole, preferred_element_type=jnp.float32)

    def rows_of(ref, at, count):
        return ref.at[pl.ds(pl.multiple_of(at * count, 8), count)]

    def gradient_sum():
        send((GRAD, 0), lambda: (grads.at[1 - c], buf0, sibling))
        wait((GRAD, 0), buf0)
        summed[...] = grads[c] + buf0[...]
        for d in FAR_FIRST:
            send((GRAD, d), lambda d=d: (rows_of(summed, (pos_a + d) % 8, 48), buf_a.at[d - 1], along_a(d)))
        total = summed[pl.ds(pl.multiple_of(pos_a * 48, 8), 48), :]
        for d in FAR_FIRST:
            wait((GRAD, d), buf_a.at[d - 1])
            total = total + buf_a[d - 1]
        mid[0:48, :] = total
        mid[48:64, :] = jnp.zeros((16, 384), jnp.float32)
        for d in FAR_FIRST:
            send((GRAD, 7 + d), lambda d=d: (rows_of(mid, (pos_b + d) % 8, 8), buf_b.at[d - 1], along_b(d)))
        total = mid[pl.ds(pl.multiple_of(pos_b * 8, 8), 8), :]
        for d in FAR_FIRST:
            wait((GRAD, 7 + d), buf_b.at[d - 1])
            total = total + buf_b[d - 1]
        buf_x[x] = total
        for d in (2, 1, 3):
            send((GRAD, 14 + d), lambda d=d: (buf_x.at[x], buf_x.at[x], along_x(d)))
        for d in (2, 1, 3):
            wait((GRAD, 14 + d), buf_x.at[(x + 4 - d) % 4])
        tail[pl.ds(pl.multiple_of(pos_b * 8, 8), 8), :] = (buf_x[0] + buf_x[1]) + (buf_x[2] + buf_x[3])
        for d in FAR_FIRST:
            send((GRAD, 17 + d), lambda d=d: (rows_of(tail, pos_b, 8), rows_of(tail, pos_b, 8), along_b(d)))
        for d in FAR_FIRST:
            wait((GRAD, 17 + d), rows_of(tail, (pos_b + 8 - d) % 8, 8))
        for d in FAR_FIRST:
            send((GRAD, 24 + d), lambda d=d: (tail.at[pl.ds(0, 48)], fin.at[c, pl.ds(pl.multiple_of(pos_a * 48, 8), 48)], along_a(d)))
        send((GRAD, 32), lambda: (tail.at[pl.ds(0, 48)], fin.at[c, pl.ds(pl.multiple_of(pos_a * 48, 8), 48)], sibling))
        fin[c, pl.ds(pl.multiple_of(pos_a * 48, 8), 48), :] = tail[0:48, :]

        def there(d, core, far):
            base = far * y + (1 - far) * z
            return fin.at[core, pl.ds(pl.multiple_of((base + 8 - d) % 8 * 48, 8), 48)]

        for d in NEAR_FIRST:
            wait((GRAD, 24 + d), there(d, c, c))
            send((GRAD, 32 + d), lambda d=d: (there(d, c, c), there(d, c, c), sibling))
        wait((GRAD, 32), there(0, 1 - c, 1 - c))
        for d in NEAR_FIRST:
            wait((GRAD, 32 + d), there(d, 1 - c, 1 - c))
        f_out[...] = fin[0]
        g_out[...] = fin[1]

    send((Z,), lambda: (pack_ref, block(O, 0, 0), z_far))
    for s in (0, 1):
        send_block((O, 1, 0, 1, s), O, 0, 0, y_dev[s])
    start_x(O, 0)
    for t in range(CHUNKS):
        own_ctx(t, 0, (0, 1, 2) if t < LEAD else (0,))
        own_ctx(t, 1, (1, 2, 3) if t < LEAD else (3,))
    for t in range(CHUNKS):
        send((CTX, 4, t, 0), lambda t=t: (mine(t), lanes(t, n), sibling))
    for copy in keep():
        copy.start()
    for key in ORDER:
        task(key)
    side_block()
    gradient_sum()
    for key, make, chips in sent:
        only(chips, lambda: remote(key, *make()).wait_send())


def fused(context, out_weight, side_down, ln_gain, residual, f_weight, g_weight, targets):
    vmem = pl.BlockSpec(memory_space=pltpu.VMEM)
    away = pl.BlockSpec(memory_space=pl.ANY)
    tall = ROWS + 8
    f32 = jnp.float32
    bf16 = jnp.bfloat16
    piece = pltpu.VMEM((CHUNKS, 4, tall, WIDTH), f32)
    square = jax.ShapeDtypeStruct((384, 384), f32)
    return pl.pallas_call(
        fused_kernel,
        out_shape=(jax.ShapeDtypeStruct((128, 768), f32), square, square),
        in_specs=[vmem] * 4 + [away] * 4,
        out_specs=(vmem, vmem, vmem),
        scratch_shapes=[
            pltpu.VMEM((64, 768), bf16),
            pltpu.VMEM((8, 128, 768), bf16),
            pltpu.VMEM((384, 384), bf16),
            pltpu.VMEM((384, 384), bf16),
            pltpu.VMEM((128, 768), f32),
            pltpu.VMEM((64, 64, 768), bf16),
            pltpu.VMEM((8, 128, 3072), bf16),
            pltpu.VMEM((768, 768), bf16),
            pltpu.VMEM((CHUNKS, 8 * ROWS, 768), f32),
            pltpu.VMEM((CHUNKS, 2, 4, tall, WIDTH), f32),
            piece,
            piece,
            piece,
            piece,
            pltpu.VMEM((136, WIDTH), f32),
            pltpu.VMEM((2, 384, 384), f32),
            pltpu.VMEM((384, 384), f32),
            pltpu.VMEM((384, 384), f32),
            pltpu.VMEM((7, 48, 384), f32),
            pltpu.VMEM((64, 384), f32),
            pltpu.VMEM((7, 8, 384), f32),
            pltpu.VMEM((4, 8, 384), f32),
            pltpu.VMEM((64, 384), f32),
            pltpu.VMEM((2, 384, 384), f32),
            pltpu.SemaphoreType.DMA((6,)),
            pltpu.SemaphoreType.DMA((SLOTS,)),
            pltpu.SemaphoreType.DMA((SLOTS,)),
        ],
        compiler_params=pltpu.CompilerParams(collective_id=0, has_side_effects=True, vmem_limit_bytes=60 * 1024 * 1024),
        name="fused_layer",
    )(
        context.reshape(8, 128, 384), out_weight, side_down.T, ln_gain.reshape(1, 768), residual.reshape(8, 128, 768),
        f_weight, g_weight, targets,
    )


def per_device(context, out_weight, residual, ln_gain, side_down, f_weight, g_weight, targets):
    return fused(context, out_weight, side_down, ln_gain, residual, f_weight, g_weight, targets)


def solution(mesh):
    in_specs = (
        P("wide", "narrow"),
        P("wide", "narrow"),
        P("wide", "narrow"),
        P("narrow"),
        P("narrow", "wide"),
        P(),
        P(),
        P(("wide", "narrow"), None),
    )
    out_specs = (P(("wide", "narrow"), None), P(), P())
    return jax.shard_map(
        per_device, mesh=mesh, in_specs=in_specs, out_specs=out_specs, check_vma=False
    )
```

```python
import math

import jax
import jax.numpy as jnp
from jax import lax
from jax.experimental import pallas as pl
from jax.experimental.pallas import tpu as pltpu
from jax.sharding import PartitionSpec as P

MESH = pl.DeviceIdType.MESH


def position():
    w = lax.axis_index("wide")
    n = lax.axis_index("narrow")
    return w // 8, (w // 2) % 4, (w % 2) * 4 + n // 2, n % 2


def device(y, x, z, c):
    return ((y * 4 + x) * 2 + z // 4, (z % 4) * 2 + c)


CHUNKS = 4
ROWS = 128 // CHUNKS
WIDTH = 768
SLOTS = 320
LEAD = 2
Z, O, PW, PD, CTX, PICK, UNIT, PROJ, PAIR, P1, P2, FIN, UP, DOWN, GRAD, STAT = range(16)
FAR_FIRST = (4, 3, 5, 2, 6, 1, 7)
NEAR_FIRST = (1, 7, 2, 6, 3, 5, 4)
TOKENS = 65536
PLANES = ((0, 1), (-1, 2), (-2, 3), (-3, 4))
SPAN = {O: (0, 64), PW: (0, 48), PD: (48, 16)}
ORDER = (
    (O, 0, 0, 1, 0), (O, 0, 0, 1, 1), (O, 1, 0, 1, 0), (O, 1, 0, 1, 1), (CTX, 0, 0, 0), (CTX, 1, 0, 0),
    (O, 0, 0, 2, 0), (O, 0, 0, 2, 1), (O, 1, 0, 2, 0), (Z,), (O, 1, 0, 2, 1), (O, 0, -1, 1, 0), (O, 0, -1, 1, 1),
    (CTX, 0, 1, 0), (CTX, 1, 1, 0), (O, 0, 1, 1, 0), (O, 0, 1, 1, 1), (PW, 1, 0, 1, 1), (O, 1, 0, 3, 0),
    (PD, 1, 0, 1, 1), (PW, 0, 0, 1, 0), (PW, 0, 0, 1, 1), (O, 0, -1, 2, 0), (PW, 1, 0, 1, 0), (O, 0, -1, 2, 1),
    (PD, 1, 0, 1, 0), (O, 1, 0, 3, 1), (CTX, 0, 0, 1), (CTX, 1, 0, 1), (O, 0, 1, 2, 0), (O, 0, 1, 2, 1),
    (O, 1, 0, 4, 0), (PW, 0, 0, 2, 1), (PW, 0, 0, 2, 0), (PW, 1, 0, 2, 1), (PD, 1, 0, 2, 1), (PW, 1, -1, 1, 0),
    (O, 0, -2, 1, 1), (O, 0, -2, 1, 0), (PD, 0, 0, 1, 1), (PW, 1, -1, 1, 1), (PD, 0, 0, 1, 0), (PW, 1, 1, 1, 0),
    (CTX, 0, 2, 0), (CTX, 1, 2, 0), (PW, 1, 1, 1, 1), (PW, 1, 0, 2, 0), (O, 0, 2, 1, 1), (O, 0, 2, 1, 0),
    (PD, 1, 0, 2, 0), (O, 1, 0, 4, 1), (PW, 1, 2, 1, 0), (O, 0, -3, 1, 1), (PW, 1, 2, 1, 1), (O, 0, -3, 1, 0),
    (PD, 0, 1, 1, 1), (CTX, 0, 1, 1), (CTX, 1, 1, 1), (PD, 0, 1, 1, 0), (PD, 0, -1, 1, 1), (PD, 0, -1, 1, 0),
    (PW, 1, -1, 2, 0), (PW, 1, 0, 3, 1), (PD, 1, 0, 3, 1), (PW, 1, 1, 2, 0), (O, 0, 3, 1, 1), (O, 0, 3, 1, 0),
    (PD, 0, 2, 1, 1), (PW, 1, -1, 2, 1), (PD, 0, 2, 1, 0), (PW, 1, 0, 3, 0), (O, 0, -2, 2, 1), (CTX, 0, 3, 0),
    (CTX, 1, 3, 0), (O, 0, -2, 2, 0), (PD, 1, 0, 3, 0), (PW, 1, 1, 2, 1), (PD, 0, 0, 2, 0), (O, 0, 2, 2, 1),
    (PICK, 0), (PD, 0, -2, 1, 1), (O, 0, 2, 2, 0), (PW, 1, 2, 2, 0), (PW, 1, 2, 2, 1), (PD, 0, -2, 1, 0),
    (PW, 1, 0, 4, 1), (PW, 1, -1, 3, 0), (O, 0, 4, 1, 1), (PW, 1, -1, 3, 1), (CTX, 0, 0, 2), (CTX, 1, 0, 2),
    (O, 0, 4, 1, 0), (O, 0, -3, 2, 1), (PW, 1, 1, 3, 0), (PD, 0, 1, 2, 1), (PICK, 1), (O, 0, -3, 2, 0),
    (PD, 0, -1, 2, 1), (PW, 1, 1, 3, 1), (PICK, -1), (PD, 0, 3, 1, 0), (PW, 1, 0, 4, 0), (PD, 0, 3, 1, 1),
    (UNIT, 0, 0), (PD, 1, 0, 4, 0), (O, 0, 3, 2, 0), (O, 0, 3, 2, 1), (PW, 1, 2, 3, 1), (PD, 0, 2, 2, 0),
    (PD, 0, -3, 1, 1), (PD, 0, -3, 1, 0), (PW, 1, 2, 3, 0), (PW, 1, -1, 4, 1), (CTX, 0, 2, 1), (CTX, 1, 2, 1),
    (PD, 0, -2, 2, 0), (PW, 1, -1, 4, 0), (O, 0, 4, 2, 1), (PW, 1, 1, 4, 0), (PD, 0, 3, 2, 1), (PW, 1, 1, 4, 1),
    (O, 0, 4, 2, 0), (PD, 0, 4, 1, 1), (PW, 1, 2, 4, 1), (PD, 0, 4, 1, 0), (PD, 0, -3, 2, 1), (PICK, 2), (PICK, -2),
    (PICK, 3), (PICK, -3), (UNIT, 1, 0), (PW, 1, 2, 4, 0), (UNIT, 2, 0), (UNIT, 3, 0), (CTX, 0, 1, 2),
    (CTX, 1, 1, 2), (PD, 0, 4, 2, 0), (PICK, 4), (PROJ, 0), (UNIT, 0, 1), (UNIT, 1, 1), (UNIT, 2, 1), (CTX, 0, 3, 1),
    (CTX, 1, 3, 1), (PAIR, 0), (UNIT, 3, 1), (PROJ, 1), (CTX, 0, 2, 2), (CTX, 1, 2, 2), (P1, 0, 0), (PAIR, 1),
    (UNIT, 0, 2), (UNIT, 1, 2), (P1, 0, 1), (UNIT, 2, 2), (CTX, 0, 3, 2), (CTX, 1, 3, 2), (UNIT, 3, 2), (P2, 0),
    (PROJ, 2), (P1, 1, 0), (UNIT, 0, 3), (UNIT, 1, 3), (UNIT, 2, 3), (P1, 1, 1), (FIN, 0), (PAIR, 2), (UNIT, 3, 3),
    (PROJ, 3), (P2, 1), (P1, 2, 0), (PAIR, 3), (P1, 2, 1), (FIN, 1), (P2, 2), (P1, 3, 0), (FIN, 2), (P1, 3, 1),
    (P2, 3), (FIN, 3),
)


def half(kind, side, flip):
    if kind == O:
        return (32 * side, 32)
    if kind == PW:
        return ((0, 32), (32, 16))[side] if flip == 0 else ((0, 16), (16, 32))[side]
    return (48, 16) if side == flip else None


def split(value):
    high = value.astype(jnp.bfloat16)
    rest = value - high.astype(jnp.float32)
    middle = rest.astype(jnp.bfloat16)
    low = (rest - middle.astype(jnp.float32)).astype(jnp.bfloat16)
    return high, middle, low


def exact_dot(value, weight, contract):
    rows = value.shape[0]
    tall = lax.dot_general(
        jnp.concatenate(split(value), axis=0), weight, (((1,), (contract,)), ((), ())), preferred_element_type=jnp.float32
    )
    return (tall[2 * rows:] + tall[rows:2 * rows]) + tall[:rows]


def gelu_and_slope(v):
    scale = math.sqrt(2.0 / math.pi)
    square = v * v
    bent = jnp.tanh(scale * (v + 0.044715 * (square * v)))
    share = 0.5 * (1.0 + bent)
    slope = share + 0.5 * v * (1.0 - bent * bent) * (scale * (1.0 + 3.0 * 0.044715 * square))
    return v * share, slope


def fused_kernel(
    ctx_hbm, weight_hbm, side_hbm, gain_hbm, res_hbm, f_hbm, g_hbm, targets_hbm, o_ref, f_out, g_out,
    ctx_ref, weight_ref, side_ref, gain_ref, pack_ref, res_ref, f_ref, g_ref, targets_ref, wbuf, cbuf, down, acc, part, pair, line, up_in, down_in, sums, columns, tiles, tiles_in, tiles_sum, tiles_far,
    grads, buf0, summed, buf_a, mid, buf_b, buf_x, tail, fin, local, send_sems, recv_sems
):
    y, x, z, c = position()
    j = z % 4
    n = j * 2 + c
    zh = z // 4
    sibling = device(y, x, z, 1 - c)
    y_dev = (device((y + 1) % 8, x, z, c), device((y + 7) % 8, x, z, c))
    x_dev = (device(y, (x + 1) % 4, z, c), device(y, (x + 3) % 4, z, c))
    z_dev = (device(y, x, (z + 1) % 8, c), device(y, x, (z + 7) % 8, c))
    chip_dev = [device(y, x, z - j + (j + d) % 4, c) for d in (1, 2, 3)]
    z_far = device(y, x, (z + 4) % 8, c)

    on_z = 1 - c
    pos_a = z * on_z + y * c
    pos_b = y * on_z + z * c

    def along_a(d):
        return device((y + d * c) % 8, x, (z + d * on_z) % 8, c)

    def along_b(d):
        return device((y + d * on_z) % 8, x, (z + d * c) % 8, c)

    def along_x(d):
        return device(y, (x + d) % 4, z, c)

    barrier = pltpu.get_barrier_semaphore()
    partners = [sibling]
    partners += [along_a(d) for d in range(1, 8)] + [along_b(d) for d in range(1, 8)] + [along_x(d) for d in range(1, 4)]
    for partner in partners:
        pl.semaphore_signal(barrier, inc=1, device_id=partner, device_id_type=MESH)
    loads = [
        pltpu.make_async_copy(src, dst, local.at[2 + i])
        for i, (src, dst) in enumerate(
            (
                (weight_hbm, weight_ref),
                (side_hbm, side_ref),
                (ctx_hbm, ctx_ref),
                (gain_hbm, gain_ref),
                (res_hbm, res_ref),
                (f_hbm, f_ref),
                (g_hbm, g_ref),
                (targets_hbm, targets_ref),
            )
        )
    ]
    for load in loads:
        load.start()
    for load in loads[:4]:
        load.wait()
    pack_ref[0:48, :] = weight_ref[...]
    pack_ref[48:64, :] = jnp.zeros((16, 768), jnp.bfloat16)
    pack_ref[48:60, :] = side_ref[...]
    pl.semaphore_wait(barrier, len(partners))

    slots = {}
    sent = []
    begun = set()
    held = []

    def remote(key, src, dst, to):
        at = slots.setdefault(key, len(slots))
        return pltpu.make_async_remote_copy(
            src_ref=src, dst_ref=dst, send_sem=send_sems.at[at], recv_sem=recv_sems.at[at], device_id=to, device_id_type=MESH
        )

    def only(chips, action):
        if chips is None:
            action()
            return
        low, high = min(chips), max(chips)
        if low == high:
            pl.when(j == low)(action)
        elif high == 3:
            pl.when(j >= low)(action)
        elif low == 0:
            pl.when(j <= high)(action)
        else:
            pl.when((j >= low) & (j <= high))(action)

    def send(key, make, chips=None):
        only(chips, lambda: remote(key, *make()).start())
        sent.append((key, make, chips))

    def wait(key, region):
        remote(key, region, region, sibling).wait_recv()

    def plane(dy):
        return (y + dy + 8) % 8

    def block(kind, dy, dx, span=None):
        start, count = span or SPAN[kind]
        side = zh if kind == O else 1 - zh
        at = (plane(dy) * 4 + (x + dx + 4) % 4) * 2 + side
        return wbuf.at[at, pl.ds(start, count)]

    def send_block(key, kind, dy, dx, to, span=None):
        if kind == O and dy == 0 and dx == 0:
            send(key, lambda: (pack_ref, block(O, 0, 0), to))
        else:
            send(key, lambda: (block(kind, dy, dx, span), block(kind, dy, dx, span), to))

    def start_x(kind, dy):
        if PW not in begun and (kind == PD or abs(dy) >= 2):
            held.append((kind, dy))
            return
        for s in (0, 1):
            send_block((kind, 0, dy, 1, s), kind, dy, 0, x_dev[s])

    def start_y(q):
        for s in (0, 1):
            send_block((PW, 1, q, 1, s), PW, 0, q, y_dev[s])

    def lanes(t, index):
        return cbuf.at[:, pl.ds(t * ROWS, ROWS), pl.ds(pl.multiple_of(index * 384, 128), 384)]

    def mine(t):
        return ctx_ref.at[:, pl.ds(t * ROWS, ROWS), :]

    def own_ctx(t, side, chips):
        send((CTX, side, t, 0), lambda: (mine(t), lanes(t, n), z_dev[side]), chips)

    def after_both(key):
        twin = key[:-1] + (1 - key[-1],)
        begun.add(key)
        return twin in begun

    def z_event(key):
        wait(key, wbuf.at[(y * 4 + x) * 2 + 1 - zh])
        for s in (0, 1):
            send_block((PW, 0, 0, 1, s), PW, 0, 0, x_dev[s])
        start_y(0)
        for s in (0, 1):
            send_block((PD, 1, 0, 1, s), PD, 0, 0, y_dev[s])
        start_x(PD, 0)

    def y_first(key):
        kind, _, _, s, side = key
        dy = (-1 if side == 0 else 1) * s
        wait(key, block(kind, dy, 0, half(kind, side, 0) if s == 4 else None))
        if s < 4:
            span = half(kind, side, 0) if s == 3 else SPAN[kind]
            if span:
                send_block((kind, 1, 0, s + 1, side), kind, dy, 0, y_dev[side], span)
            start_x(kind, dy)
        elif kind == PD or after_both(key):
            start_x(kind, 4)

    def x_second(key):
        kind, _, dy, s, side = key
        dx = (-1 if side == 0 else 1) * s
        span = half(kind, side, dy % 2)
        wait(key, block(kind, dy, dx, span if s == 2 else None))
        if s == 1 and span:
            send_block((kind, 0, dy, 2, side), kind, dy, dx, x_dev[side], span)

    def x_first(key):
        _, _, _, s, side = key
        dx = (-1 if side == 0 else 1) * s
        span = half(PW, side, 0)
        wait(key, block(PW, 0, dx, span if s == 2 else None))
        if s == 1:
            send_block((PW, 0, 0, 2, side), PW, 0, dx, x_dev[side], span)
            start_y(dx)
            if after_both(key):
                begun.add(PW)
                for item in held:
                    start_x(*item)
        elif after_both(key):
            start_y(2)

    def y_second(key):
        _, _, q, s, side = key
        dy = (-1 if side == 0 else 1) * s
        span = half(PW, side, q % 2)
        wait(key, block(PW, dy, q, span if s == 4 else None))
        if s < 4:
            send_block((PW, 1, q, s + 1, side), PW, dy, q, y_dev[side], span if s == 3 else None)

    def reach(side, h):
        return range(1 + h, 4) if side == 0 else range(0, 3 - h)

    def source(side, h):
        return j + (-1 if side == 0 else 1) * (1 + h)

    def ctx_event(key):
        _, side, t, h = key
        chips = reach(side, h)
        region = lambda: lanes(t, source(side, h) * 2 + c)
        onward = [k for k in chips if (k < 3 if side == 0 else k > 0)]
        further = (CTX, side, t, h + 1), lambda: (region(), region(), z_dev[side]), onward
        share = (CTX, side + 2, t, h), lambda: (region(), region(), sibling), chips

        def arrived():
            wait(key, region())
            if onward:
                only(onward, lambda: remote(further[0], *further[1]()).start())
            remote(share[0], *share[1]()).start()

        only(chips, arrived)
        sent.extend([further, share] if onward else [share])
        if h == 0 and t + LEAD < CHUNKS:
            own_ctx(t + LEAD, side, (1, 2))

    def keep():
        return pltpu.make_async_copy(pack_ref, block(O, 0, 0), local.at[0]), pltpu.make_async_copy(
            ctx_ref, cbuf.at[:, :, pl.ds(pl.multiple_of(n * 384, 128), 384)], local.at[1]
        )

    def pick(key):
        if PICK not in begun:
            begun.add(PICK)
            for copy in keep():
                copy.wait()
        lane = lax.broadcasted_iota(jnp.int32, (96, 128), 1)
        row = lax.broadcasted_iota(jnp.int32, (96, 128), 0)
        here = ((lane & 15) < 12) & ((lane >> 4) * 12 + (lane & 15) == row)
        chosen = jnp.where(here, 1.0, 0.0).astype(jnp.bfloat16)
        k = plane(key[1])
        padded = wbuf[pl.ds(pl.multiple_of(k * 8, 8), 8), 48:64, :].reshape(128, 768)
        picked = jnp.dot(chosen, padded, preferred_element_type=jnp.float32)
        down[pl.ds(pl.multiple_of(k * 96, 32), 96), :] = picked.astype(jnp.bfloat16)

    def unit(key):
        _, p, t = key
        if (CTX, t) not in begun:
            begun.add((CTX, t))
            for h in range(3):
                for side in (0, 1):
                    only(reach(side, h), lambda: wait((CTX, side + 2, t, h), lanes(t, source(side, h) * 2 + 1 - c)))
            wait((CTX, 4, t, 0), lanes(t, j * 2 + 1 - c))
        here = pl.ds(t * ROWS, ROWS)
        ks = [plane(dy) for dy in PLANES[p]]
        lhs = [cbuf[:, here, pl.ds(pl.multiple_of(k * 384, 128), 384)].reshape(8 * ROWS, 384) for k in ks]
        rhs = [wbuf[pl.ds(pl.multiple_of(k * 8, 8), 8), 0:48, :].reshape(384, 768) for k in ks]
        product = jnp.dot(
            jnp.concatenate(lhs, axis=1), jnp.concatenate(rhs, axis=0), preferred_element_type=jnp.float32
        )
        if (UNIT, t) in begun:
            acc[t] += product
        else:
            begun.add((UNIT, t))
            acc[t] = product

    def project(key):
        t = key[1]
        here = pl.ds(t * ROWS, ROWS)
        if PROJ not in begun:
            begun.add(PROJ)
            loads[4].wait()
        gain = gain_ref[...].astype(jnp.float32).reshape(1, 768)
        stream = (res_ref[:, here, :].reshape(8 * ROWS, 768).astype(jnp.float32) + acc[t]).astype(jnp.bfloat16)
        value = stream.astype(jnp.float32)
        total = jnp.sum(value, axis=1, keepdims=True)
        squares = jnp.sum(value * value, axis=1, keepdims=True)
        scaled = (value * gain).astype(jnp.bfloat16)
        mapped = lax.dot_general(scaled, down[...], (((1,), (1,)), ((), ())), preferred_element_type=jnp.float32)
        column = lax.broadcasted_iota(jnp.int32, (8 * ROWS, 128), 1)
        stats = jnp.where(column == 0, total, jnp.where(column == 1, squares, 0.0))
        for k in range(8):
            cut = slice(k * ROWS, (k + 1) * ROWS)
            part[t, k % 2, k // 2] = mapped[cut]
            columns[k, here, :] = stats[cut]
        begun.add((PROJ, t))
        send((PAIR, t), lambda: (part.at[t, 1 - c], pair.at[t], sibling))
        if all((PROJ, k) in begun for k in range(CHUNKS)):
            stats_start(gain)

    def stats_start(gain):
        rows = jnp.broadcast_to(gain, (16, 768)).astype(jnp.bfloat16)
        shares = lax.dot_general(rows, down[...], (((1,), (1,)), ((), ())), preferred_element_type=jnp.float32)
        row = lax.broadcasted_iota(jnp.int32, (8, 128), 0)
        lower = jnp.zeros((8, 128), jnp.float32)
        for i in range(6):
            lower = jnp.where(row == i + 2, shares[0:8, i * 128:(i + 1) * 128], lower)
        for k in range(8):
            tiles[k % 2, k // 2] = jnp.where(row < 2, jnp.transpose(columns[k])[0:8, :], lower)
        send((STAT, 0), lambda: (tiles.at[1 - c], tiles_in, sibling))

    def stats_pass():
        wait((STAT, 0), tiles_in)
        tiles_sum[...] = tiles[c] + tiles_in[...]
        for d in (2, 1, 3):
            send((STAT, d), lambda d=d: (tiles_sum.at[(j + d) % 4], tiles_far.at[d - 1], chip_dev[d - 1]))

    def stats_end():
        total = tiles_sum[j]
        for d in (2, 1, 3):
            wait((STAT, d), tiles_far.at[d - 1])
            total = total + tiles_far[d - 1]
        return jnp.transpose(jnp.concatenate([total, jnp.zeros((120, 128), jnp.float32)], axis=0)), jnp.concatenate(
            [total[i + 2:i + 3, :] for i in range(6)], axis=1
        )

    def piece(ref, t, dest):
        return ref.at[t, dest]

    def add_pair(key):
        t = key[1]
        wait(key, pair.at[t])
        line[t] = part[t, c] + pair[t]
        for i in range(3):
            pass_on(t, 0, 0, 3 - i, True)
            pass_on(t, 3, 1, i, True)
        begun.add(key)
        if all((PAIR, k) in begun for k in range(CHUNKS)):
            stats_pass()

    def pass_on(t, chip, side, dest, first=False):
        kind, arrived = ((UP, up_in), (DOWN, down_in))[side]
        if not first:

            def add():
                wait((kind, t, dest), piece(arrived, t, dest))
                line[t, dest] += arrived[t, dest]

            only((chip,), add)
        send((kind, t, dest), lambda: (piece(line, t, dest), piece(arrived, t, dest), z_dev[side]), (chip,))

    def finish(key):
        t = key[1]
        for chip in range(4):

            def add():
                total = line[t, chip]
                if chip > 0:
                    wait((UP, t, chip), piece(up_in, t, chip))
                    total = total + up_in[t, chip]
                if chip < 3:
                    wait((DOWN, t, chip), piece(down_in, t, chip))
                    total = total + down_in[t, chip]
                sums[t * ROWS:(t + 1) * ROWS, :] = total

            only((chip,), add)

    def task(key):
        kind = key[0]
        if kind == Z:
            z_event(key)
        elif kind in (O, PD):
            (y_first if key[1] else x_second)(key)
        elif kind == PW:
            (y_second if key[1] else x_first)(key)
        elif kind == CTX:
            ctx_event(key)
        elif kind == P1:
            _, t, i = key
            pass_on(t, 1, 0, 3 - i)
            pass_on(t, 2, 1, i)
        elif kind == P2:
            pass_on(key[1], 2, 0, 3)
            pass_on(key[1], 1, 1, 0)
        else:
            {PICK: pick, UNIT: unit, PROJ: project, PAIR: add_pair, FIN: finish}[kind](key)

    def drain():
        for key, make, chips in sent:
            only(chips, lambda: remote(key, *make()).wait_send())
        sent.clear()

    def side_block():
        for load in loads[5:]:
            load.wait()
        stats, gain_map = stats_end()
        mean = stats[:, 0:1] * (1.0 / (8 * 768))
        spread = stats[:, 1:2] * (1.0 / (8 * 768)) - mean * mean
        scale = 1.0 / jnp.sqrt(spread + 1e-06)
        first = (sums[0:128, 0:384] - mean * gain_map[:, 0:384]) * scale
        second = (sums[0:128, 384:768] - mean * gain_map[:, 384:768]) * scale
        bend, f_slope = gelu_and_slope(exact_dot(second, f_ref[...], 0))
        upper = first + bend
        bend, g_slope = gelu_and_slope(exact_dot(upper, g_ref[...], 0))
        lower = second + bend
        o_ref[:, 0:384] = upper
        o_ref[:, 384:768] = lower
        back = (lower - targets_ref[:, 384:768]) * (1.0 / TOKENS) * g_slope
        upper_total = (upper - targets_ref[:, 0:384]) * (1.0 / TOKENS) + exact_dot(back, g_ref[...], 1)
        whole = lax.Precision.HIGHEST
        over_tokens = (((0,), (0,)), ((), ()))
        grads[1] = lax.dot_general(upper, back, over_tokens, precision=whole, preferred_element_type=jnp.float32)
        grads[0] = lax.dot_general(second, upper_total * f_slope, over_tokens, precision=whole, preferred_element_type=jnp.float32)

    def rows_of(ref, at, count):
        return ref.at[pl.ds(pl.multiple_of(at * count, 8), count)]

    def gradient_sum():
        send((GRAD, 0), lambda: (grads.at[1 - c], buf0, sibling))
        wait((GRAD, 0), buf0)
        summed[...] = grads[c] + buf0[...]
        for d in FAR_FIRST:
            send((GRAD, d), lambda d=d: (rows_of(summed, (pos_a + d) % 8, 48), buf_a.at[d - 1], along_a(d)))
        earlier, later = sent[:-8], sent[-8:]
        sent[:] = earlier
        drain()
        sent.extend(later)
        total = summed[pl.ds(pl.multiple_of(pos_a * 48, 8), 48), :]
        for d in FAR_FIRST:
            wait((GRAD, d), buf_a.at[d - 1])
            total = total + buf_a[d - 1]
        mid[0:48, :] = total
        mid[48:64, :] = jnp.zeros((16, 384), jnp.float32)
        for d in FAR_FIRST:
            send((GRAD, 7 + d), lambda d=d: (rows_of(mid, (pos_b + d) % 8, 8), buf_b.at[d - 1], along_b(d)))
        total = mid[pl.ds(pl.multiple_of(pos_b * 8, 8), 8), :]
        for d in FAR_FIRST:
            wait((GRAD, 7 + d), buf_b.at[d - 1])
            total = total + buf_b[d - 1]
        buf_x[x] = total
        for d in (2, 1, 3):
            send((GRAD, 14 + d), lambda d=d: (buf_x.at[x], buf_x.at[x], along_x(d)))
        for d in (2, 1, 3):
            wait((GRAD, 14 + d), buf_x.at[(x + 4 - d) % 4])
        tail[pl.ds(pl.multiple_of(pos_b * 8, 8), 8), :] = (buf_x[0] + buf_x[1]) + (buf_x[2] + buf_x[3])
        for d in FAR_FIRST:
            send((GRAD, 17 + d), lambda d=d: (rows_of(tail, pos_b, 8), rows_of(tail, pos_b, 8), along_b(d)))
        for d in FAR_FIRST:
            wait((GRAD, 17 + d), rows_of(tail, (pos_b + 8 - d) % 8, 8))
        for d in FAR_FIRST:
            send((GRAD, 24 + d), lambda d=d: (tail.at[pl.ds(0, 48)], fin.at[c, pl.ds(pl.multiple_of(pos_a * 48, 8), 48)], along_a(d)))
        send((GRAD, 32), lambda: (tail.at[pl.ds(0, 48)], fin.at[c, pl.ds(pl.multiple_of(pos_a * 48, 8), 48)], sibling))
        fin[c, pl.ds(pl.multiple_of(pos_a * 48, 8), 48), :] = tail[0:48, :]

        def there(d, core, far):
            base = far * y + (1 - far) * z
            return fin.at[core, pl.ds(pl.multiple_of((base + 8 - d) % 8 * 48, 8), 48)]

        for d in NEAR_FIRST:
            wait((GRAD, 24 + d), there(d, c, c))
            send((GRAD, 32 + d), lambda d=d: (there(d, c, c), there(d, c, c), sibling))
        wait((GRAD, 32), there(0, 1 - c, 1 - c))
        for d in NEAR_FIRST:
            wait((GRAD, 32 + d), there(d, 1 - c, 1 - c))
        f_out[...] = fin[0]
        g_out[...] = fin[1]

    send((Z,), lambda: (pack_ref, block(O, 0, 0), z_far))
    for s in (0, 1):
        send_block((O, 1, 0, 1, s), O, 0, 0, y_dev[s])
    start_x(O, 0)
    for t in range(CHUNKS):
        own_ctx(t, 0, (0, 1, 2) if t < LEAD else (0,))
        own_ctx(t, 1, (1, 2, 3) if t < LEAD else (3,))
    for t in range(CHUNKS):
        send((CTX, 4, t, 0), lambda t=t: (mine(t), lanes(t, n), sibling))
    for copy in keep():
        copy.start()
    for key in ORDER:
        task(key)
    side_block()
    gradient_sum()
    drain()


def fused(context, out_weight, side_down, ln_gain, residual, f_weight, g_weight, targets):
    vmem = pl.BlockSpec(memory_space=pltpu.VMEM)
    away = pl.BlockSpec(memory_space=pltpu.HBM)
    f32 = jnp.float32
    bf16 = jnp.bfloat16
    piece = pltpu.VMEM((CHUNKS, 4, ROWS, WIDTH), f32)
    square = jax.ShapeDtypeStruct((384, 384), f32)
    return pl.pallas_call(
        fused_kernel,
        out_shape=(jax.ShapeDtypeStruct((128, 768), f32), square, square),
        in_specs=[away] * 8,
        out_specs=(vmem, vmem, vmem),
        scratch_shapes=[
            pltpu.VMEM((8, 128, 384), bf16),
            pltpu.VMEM((48, 768), bf16),
            pltpu.VMEM((12, 768), bf16),
            pltpu.VMEM((768,), bf16),
            pltpu.VMEM((64, 768), bf16),
            pltpu.VMEM((8, 128, 768), bf16),
            pltpu.VMEM((384, 384), bf16),
            pltpu.VMEM((384, 384), bf16),
            pltpu.VMEM((128, 768), f32),
            pltpu.VMEM((64, 64, 768), bf16),
            pltpu.VMEM((8, 128, 3072), bf16),
            pltpu.VMEM((768, 768), bf16),
            pltpu.VMEM((CHUNKS, 8 * ROWS, 768), f32),
            pltpu.VMEM((CHUNKS, 2, 4, ROWS, WIDTH), f32),
            piece,
            piece,
            piece,
            piece,
            pltpu.VMEM((128, WIDTH), f32),
            pltpu.VMEM((8, 128, 128), f32),
            pltpu.VMEM((2, 4, 8, 128), f32),
            pltpu.VMEM((4, 8, 128), f32),
            pltpu.VMEM((4, 8, 128), f32),
            pltpu.VMEM((3, 8, 128), f32),
            pltpu.VMEM((2, 384, 384), f32),
            pltpu.VMEM((384, 384), f32),
            pltpu.VMEM((384, 384), f32),
            pltpu.VMEM((7, 48, 384), f32),
            pltpu.VMEM((64, 384), f32),
            pltpu.VMEM((7, 8, 384), f32),
            pltpu.VMEM((4, 8, 384), f32),
            pltpu.VMEM((64, 384), f32),
            pltpu.VMEM((2, 384, 384), f32),
            pltpu.SemaphoreType.DMA((10,)),
            pltpu.SemaphoreType.DMA((SLOTS,)),
            pltpu.SemaphoreType.DMA((SLOTS,)),
        ],
        compiler_params=pltpu.CompilerParams(collective_id=0, has_side_effects=True, vmem_limit_bytes=60 * 1024 * 1024),
        name="fused_layer",
    )(
        context.reshape(8, 128, 384), out_weight, side_down.T, ln_gain, residual.reshape(8, 128, 768),
        f_weight, g_weight, targets,
    )


def hand_over(a_ref, b_ref, c_ref, a_out, b_out, c_out, a_kept, b_kept, c_kept, sems):
    steps = [
        (pltpu.make_async_copy(src, kept, sems.at[0, i]), pltpu.make_async_copy(kept, dst, sems.at[1, i]))
        for i, (src, kept, dst) in enumerate(
            ((a_ref, a_kept, a_out), (b_ref, b_kept, b_out), (c_ref, c_kept, c_out))
        )
    ]
    for load, _ in steps:
        load.start()
    for load, store in steps:
        load.wait()
        store.start()
    for _, store in steps:
        store.wait()


def per_device(context, out_weight, residual, ln_gain, side_down, f_weight, g_weight, targets):
    results = fused(context, out_weight, side_down, ln_gain, residual, f_weight, g_weight, targets)
    away = pl.BlockSpec(memory_space=pltpu.HBM)
    return pl.pallas_call(
        hand_over,
        out_shape=tuple(jax.ShapeDtypeStruct(r.shape, r.dtype) for r in results),
        in_specs=[away] * 3,
        out_specs=(away,) * 3,
        scratch_shapes=[pltpu.VMEM(r.shape, r.dtype) for r in results] + [pltpu.SemaphoreType.DMA((2, 3))],
        name="hand_over",
    )(*results)


def solution(mesh):
    in_specs = (
        P("wide", "narrow"),
        P("wide", "narrow"),
        P("wide", "narrow"),
        P("narrow"),
        P("narrow", "wide"),
        P(),
        P(),
        P(("wide", "narrow"), None),
    )
    out_specs = (P(("wide", "narrow"), None), P(), P())
    return jax.shard_map(
        per_device, mesh=mesh, in_specs=in_specs, out_specs=out_specs, check_vma=False
    )
```

```python
import math

import jax
import jax.numpy as jnp
from jax import lax
from jax.experimental import pallas as pl
from jax.experimental.pallas import tpu as pltpu
from jax.sharding import PartitionSpec as P

MESH = pl.DeviceIdType.MESH


def position():
    w = lax.axis_index("wide")
    n = lax.axis_index("narrow")
    return w // 8, (w // 2) % 4, (w % 2) * 4 + n // 2, n % 2


def device(y, x, z, c):
    return ((y * 4 + x) * 2 + z // 4, (z % 4) * 2 + c)


CHUNKS = 4
ROWS = 128 // CHUNKS
WIDTH = 768
SLOTS = 320
LEAD = 2
Z, O, PW, PD, CTX, PICK, UNIT, PROJ, PAIR, P1, P2, FIN, UP, DOWN, GRAD, STAT = range(16)
FAR_FIRST = (4, 3, 5, 2, 6, 1, 7)
NEAR_FIRST = (1, 7, 2, 6, 3, 5, 4)
TOKENS = 65536
PLANES = ((0, 1), (-1, 2), (-2, 3), (-3, 4))
SPAN = {O: (0, 64), PW: (0, 48), PD: (48, 16)}
ORDER = (
    (O, 0, 0, 1, 0), (O, 0, 0, 1, 1), (O, 1, 0, 1, 0), (O, 1, 0, 1, 1), (CTX, 0, 0, 0), (CTX, 1, 0, 0),
    (O, 0, 0, 2, 0), (O, 0, 0, 2, 1), (O, 1, 0, 2, 0), (Z,), (O, 1, 0, 2, 1), (O, 0, -1, 1, 0), (O, 0, -1, 1, 1),
    (CTX, 0, 1, 0), (CTX, 1, 1, 0), (O, 0, 1, 1, 0), (O, 0, 1, 1, 1), (PW, 1, 0, 1, 1), (O, 1, 0, 3, 0),
    (PD, 1, 0, 1, 1), (PW, 0, 0, 1, 0), (PW, 0, 0, 1, 1), (O, 0, -1, 2, 0), (PW, 1, 0, 1, 0), (O, 0, -1, 2, 1),
    (PD, 1, 0, 1, 0), (O, 1, 0, 3, 1), (CTX, 0, 0, 1), (CTX, 1, 0, 1), (O, 0, 1, 2, 0), (O, 0, 1, 2, 1),
    (O, 1, 0, 4, 0), (PW, 0, 0, 2, 1), (PW, 0, 0, 2, 0), (PW, 1, 0, 2, 1), (PD, 1, 0, 2, 1), (PW, 1, -1, 1, 0),
    (O, 0, -2, 1, 1), (O, 0, -2, 1, 0), (PD, 0, 0, 1, 1), (PW, 1, -1, 1, 1), (PD, 0, 0, 1, 0), (PW, 1, 1, 1, 0),
    (CTX, 0, 2, 0), (CTX, 1, 2, 0), (PW, 1, 1, 1, 1), (PW, 1, 0, 2, 0), (O, 0, 2, 1, 1), (O, 0, 2, 1, 0),
    (PD, 1, 0, 2, 0), (O, 1, 0, 4, 1), (PW, 1, 2, 1, 0), (O, 0, -3, 1, 1), (PW, 1, 2, 1, 1), (O, 0, -3, 1, 0),
    (PD, 0, 1, 1, 1), (CTX, 0, 1, 1), (CTX, 1, 1, 1), (PD, 0, 1, 1, 0), (PD, 0, -1, 1, 1), (PD, 0, -1, 1, 0),
    (PW, 1, -1, 2, 0), (PW, 1, 0, 3, 1), (PD, 1, 0, 3, 1), (PW, 1, 1, 2, 0), (O, 0, 3, 1, 1), (O, 0, 3, 1, 0),
    (PD, 0, 2, 1, 1), (PW, 1, -1, 2, 1), (PD, 0, 2, 1, 0), (PW, 1, 0, 3, 0), (O, 0, -2, 2, 1), (CTX, 0, 3, 0),
    (CTX, 1, 3, 0), (O, 0, -2, 2, 0), (PD, 1, 0, 3, 0), (PW, 1, 1, 2, 1), (PD, 0, 0, 2, 0), (O, 0, 2, 2, 1),
    (PICK, 0), (PD, 0, -2, 1, 1), (O, 0, 2, 2, 0), (PW, 1, 2, 2, 0), (PW, 1, 2, 2, 1), (PD, 0, -2, 1, 0),
    (PW, 1, 0, 4, 1), (PW, 1, -1, 3, 0), (O, 0, 4, 1, 1), (PW, 1, -1, 3, 1), (CTX, 0, 0, 2), (CTX, 1, 0, 2),
    (O, 0, 4, 1, 0), (O, 0, -3, 2, 1), (PW, 1, 1, 3, 0), (PD, 0, 1, 2, 1), (PICK, 1), (O, 0, -3, 2, 0),
    (PD, 0, -1, 2, 1), (PW, 1, 1, 3, 1), (PICK, -1), (PD, 0, 3, 1, 0), (PW, 1, 0, 4, 0), (PD, 0, 3, 1, 1),
    (UNIT, 0, 0), (PD, 1, 0, 4, 0), (O, 0, 3, 2, 0), (O, 0, 3, 2, 1), (PW, 1, 2, 3, 1), (PD, 0, 2, 2, 0),
    (PD, 0, -3, 1, 1), (PD, 0, -3, 1, 0), (PW, 1, 2, 3, 0), (PW, 1, -1, 4, 1), (CTX, 0, 2, 1), (CTX, 1, 2, 1),
    (PD, 0, -2, 2, 0), (PW, 1, -1, 4, 0), (O, 0, 4, 2, 1), (PW, 1, 1, 4, 0), (PD, 0, 3, 2, 1), (PW, 1, 1, 4, 1),
    (O, 0, 4, 2, 0), (PD, 0, 4, 1, 1), (PW, 1, 2, 4, 1), (PD, 0, 4, 1, 0), (PD, 0, -3, 2, 1), (PICK, 2), (PICK, -2),
    (PICK, 3), (PICK, -3), (UNIT, 1, 0), (PW, 1, 2, 4, 0), (UNIT, 2, 0), (UNIT, 3, 0), (CTX, 0, 1, 2),
    (CTX, 1, 1, 2), (PD, 0, 4, 2, 0), (PICK, 4), (PROJ, 0), (UNIT, 0, 1), (UNIT, 1, 1), (UNIT, 2, 1), (CTX, 0, 3, 1),
    (CTX, 1, 3, 1), (PAIR, 0), (UNIT, 3, 1), (PROJ, 1), (CTX, 0, 2, 2), (CTX, 1, 2, 2), (P1, 0, 0), (PAIR, 1),
    (UNIT, 0, 2), (UNIT, 1, 2), (P1, 0, 1), (UNIT, 2, 2), (CTX, 0, 3, 2), (CTX, 1, 3, 2), (UNIT, 3, 2), (P2, 0),
    (PROJ, 2), (P1, 1, 0), (UNIT, 0, 3), (UNIT, 1, 3), (UNIT, 2, 3), (P1, 1, 1), (FIN, 0), (PAIR, 2), (UNIT, 3, 3),
    (PROJ, 3), (P2, 1), (P1, 2, 0), (PAIR, 3), (P1, 2, 1), (FIN, 1), (P2, 2), (P1, 3, 0), (FIN, 2), (P1, 3, 1),
    (P2, 3), (FIN, 3),
)


def half(kind, side, flip):
    if kind == O:
        return (32 * side, 32)
    if kind == PW:
        return ((0, 32), (32, 16))[side] if flip == 0 else ((0, 16), (16, 32))[side]
    return (48, 16) if side == flip else None


def split(value):
    high = value.astype(jnp.bfloat16)
    rest = value - high.astype(jnp.float32)
    middle = rest.astype(jnp.bfloat16)
    low = (rest - middle.astype(jnp.float32)).astype(jnp.bfloat16)
    return high, middle, low


def exact_dot(value, weight, contract):
    rows = value.shape[0]
    tall = lax.dot_general(
        jnp.concatenate(split(value), axis=0), weight, (((1,), (contract,)), ((), ())), preferred_element_type=jnp.float32
    )
    return (tall[2 * rows:] + tall[rows:2 * rows]) + tall[:rows]


def gelu_and_slope(v):
    scale = math.sqrt(2.0 / math.pi)
    square = v * v
    bent = jnp.tanh(scale * (v + 0.044715 * (square * v)))
    share = 0.5 * (1.0 + bent)
    slope = share + 0.5 * v * (1.0 - bent * bent) * (scale * (1.0 + 3.0 * 0.044715 * square))
    return v * share, slope


def fused_kernel(
    ctx_hbm, weight_hbm, side_hbm, gain_hbm, res_hbm, f_hbm, g_hbm, targets_hbm, o_ref, f_out, g_out,
    ctx_ref, weight_ref, side_ref, gain_ref, pack_ref, res_ref, f_ref, g_ref, targets_ref, wbuf, cbuf, down, acc, part, pair, line, up_in, down_in, sums, columns, tiles, tiles_in, tiles_sum, tiles_far,
    grads, buf0, summed, buf_a, mid, buf_b, buf_x, tail, fin, local, send_sems, recv_sems
):
    y, x, z, c = position()
    j = z % 4
    n = j * 2 + c
    zh = z // 4
    sibling = device(y, x, z, 1 - c)
    y_dev = (device((y + 1) % 8, x, z, c), device((y + 7) % 8, x, z, c))
    x_dev = (device(y, (x + 1) % 4, z, c), device(y, (x + 3) % 4, z, c))
    z_dev = (device(y, x, (z + 1) % 8, c), device(y, x, (z + 7) % 8, c))
    chip_dev = [device(y, x, z - j + (j + d) % 4, c) for d in (1, 2, 3)]
    z_far = device(y, x, (z + 4) % 8, c)

    on_z = 1 - c
    pos_a = z * on_z + y * c
    pos_b = y * on_z + z * c

    def along_a(d):
        return device((y + d * c) % 8, x, (z + d * on_z) % 8, c)

    def along_b(d):
        return device((y + d * on_z) % 8, x, (z + d * c) % 8, c)

    def along_x(d):
        return device(y, (x + d) % 4, z, c)

    barrier = pltpu.get_barrier_semaphore()
    partners = [sibling]
    partners += [along_a(d) for d in range(1, 8)] + [along_b(d) for d in range(1, 8)] + [along_x(d) for d in range(1, 4)]
    for partner in partners:
        pl.semaphore_signal(barrier, inc=1, device_id=partner, device_id_type=MESH)
    loads = [
        pltpu.make_async_copy(src, dst, local.at[2 + i])
        for i, (src, dst) in enumerate(
            (
                (weight_hbm, weight_ref),
                (side_hbm, side_ref),
                (ctx_hbm, ctx_ref),
                (gain_hbm, gain_ref),
                (res_hbm, res_ref),
                (f_hbm, f_ref),
                (g_hbm, g_ref),
                (targets_hbm, targets_ref),
            )
        )
    ]
    for load in loads:
        load.start()
    for load in loads[:4]:
        load.wait()
    pack_ref[0:48, :] = weight_ref[...]
    pack_ref[48:64, :] = jnp.zeros((16, 768), jnp.bfloat16)
    pack_ref[48:60, :] = side_ref[...]
    pl.semaphore_wait(barrier, len(partners))

    slots = {}
    sent = []
    begun = set()
    held = []

    def remote(key, src, dst, to):
        at = slots.setdefault(key, len(slots))
        return pltpu.make_async_remote_copy(
            src_ref=src, dst_ref=dst, send_sem=send_sems.at[at], recv_sem=recv_sems.at[at], device_id=to, device_id_type=MESH
        )

    def only(chips, action):
        if chips is None:
            action()
            return
        if callable(chips):
            pl.when(chips())(action)
            return
        low, high = min(chips), max(chips)
        if low == high:
            pl.when(j == low)(action)
        elif high == 3:
            pl.when(j >= low)(action)
        elif low == 0:
            pl.when(j <= high)(action)
        else:
            pl.when((j >= low) & (j <= high))(action)

    def send(key, make, chips=None):
        only(chips, lambda: remote(key, *make()).start())
        sent.append((key, make, chips))

    def wait(key, region):
        remote(key, region, region, sibling).wait_recv()

    def plane(dy):
        return (y + dy + 8) % 8

    def block(kind, dy, dx, span=None):
        start, count = span or SPAN[kind]
        side = zh if kind == O else 1 - zh
        at = (plane(dy) * 4 + (x + dx + 4) % 4) * 2 + side
        return wbuf.at[at, pl.ds(start, count)]

    def send_block(key, kind, dy, dx, to, span=None):
        if kind == O and dy == 0 and dx == 0:
            send(key, lambda: (pack_ref, block(O, 0, 0), to))
        else:
            send(key, lambda: (block(kind, dy, dx, span), block(kind, dy, dx, span), to))

    def start_x(kind, dy):
        if PW not in begun and (kind == PD or abs(dy) >= 2):
            held.append((kind, dy))
            return
        for s in (0, 1):
            send_block((kind, 0, dy, 1, s), kind, dy, 0, x_dev[s])

    def start_y(q):
        for s in (0, 1):
            send_block((PW, 1, q, 1, s), PW, 0, q, y_dev[s])

    def lanes(t, index):
        return cbuf.at[:, pl.ds(t * ROWS, ROWS), pl.ds(pl.multiple_of(index * 384, 128), 384)]

    def mine(t):
        return ctx_ref.at[:, pl.ds(t * ROWS, ROWS), :]

    def own_ctx(t, side, chips):
        send((CTX, side, t, 0), lambda: (mine(t), lanes(t, n), z_dev[side]), chips)

    def after_both(key):
        twin = key[:-1] + (1 - key[-1],)
        begun.add(key)
        return twin in begun

    def z_event(key):
        wait(key, wbuf.at[(y * 4 + x) * 2 + 1 - zh])
        for s in (0, 1):
            send_block((PW, 0, 0, 1, s), PW, 0, 0, x_dev[s])
        start_y(0)
        for s in (0, 1):
            send_block((PD, 1, 0, 1, s), PD, 0, 0, y_dev[s])
        start_x(PD, 0)

    def y_first(key):
        kind, _, _, s, side = key
        dy = (-1 if side == 0 else 1) * s
        wait(key, block(kind, dy, 0, half(kind, side, 0) if s == 4 else None))
        if s < 4:
            span = half(kind, side, 0) if s == 3 else SPAN[kind]
            if span:
                send_block((kind, 1, 0, s + 1, side), kind, dy, 0, y_dev[side], span)
            start_x(kind, dy)
        elif kind == PD or after_both(key):
            start_x(kind, 4)

    def x_second(key):
        kind, _, dy, s, side = key
        dx = (-1 if side == 0 else 1) * s
        span = half(kind, side, dy % 2)
        wait(key, block(kind, dy, dx, span if s == 2 else None))
        if s == 1 and span:
            send_block((kind, 0, dy, 2, side), kind, dy, dx, x_dev[side], span)

    def x_first(key):
        _, _, _, s, side = key
        dx = (-1 if side == 0 else 1) * s
        span = half(PW, side, 0)
        wait(key, block(PW, 0, dx, span if s == 2 else None))
        if s == 1:
            send_block((PW, 0, 0, 2, side), PW, 0, dx, x_dev[side], span)
            start_y(dx)
            if after_both(key):
                begun.add(PW)
                for item in held:
                    start_x(*item)
        elif after_both(key):
            start_y(2)

    def y_second(key):
        _, _, q, s, side = key
        dy = (-1 if side == 0 else 1) * s
        span = half(PW, side, q % 2)
        wait(key, block(PW, dy, q, span if s == 4 else None))
        if s < 4:
            send_block((PW, 1, q, s + 1, side), PW, dy, q, y_dev[side], span if s == 3 else None)

    def reach(side, h):
        return range(1 + h, 4) if side == 0 else range(0, 3 - h)

    def source(side, h):
        return j + (-1 if side == 0 else 1) * (1 + h)

    def ctx_event(key):
        _, side, t, h = key
        chips = reach(side, h)
        region = lambda: lanes(t, source(side, h) * 2 + c)
        onward = [k for k in chips if (k < 3 if side == 0 else k > 0)]
        further = (CTX, side, t, h + 1), lambda: (region(), region(), z_dev[side]), onward
        share = (CTX, side + 2, t, h), lambda: (region(), region(), sibling), chips

        def arrived():
            wait(key, region())
            if onward:
                only(onward, lambda: remote(further[0], *further[1]()).start())
            remote(share[0], *share[1]()).start()

        only(chips, arrived)
        sent.extend([further, share] if onward else [share])
        if h == 0 and t + LEAD < CHUNKS:
            own_ctx(t + LEAD, side, (1, 2))

    def keep():
        return pltpu.make_async_copy(pack_ref, block(O, 0, 0), local.at[0]), pltpu.make_async_copy(
            ctx_ref, cbuf.at[:, :, pl.ds(pl.multiple_of(n * 384, 128), 384)], local.at[1]
        )

    def pick(key):
        if PICK not in begun:
            begun.add(PICK)
            for copy in keep():
                copy.wait()
        lane = lax.broadcasted_iota(jnp.int32, (96, 128), 1)
        row = lax.broadcasted_iota(jnp.int32, (96, 128), 0)
        here = ((lane & 15) < 12) & ((lane >> 4) * 12 + (lane & 15) == row)
        chosen = jnp.where(here, 1.0, 0.0).astype(jnp.bfloat16)
        k = plane(key[1])
        padded = wbuf[pl.ds(pl.multiple_of(k * 8, 8), 8), 48:64, :].reshape(128, 768)
        picked = jnp.dot(chosen, padded, preferred_element_type=jnp.float32)
        down[pl.ds(pl.multiple_of(k * 96, 32), 96), :] = picked.astype(jnp.bfloat16)

    def unit(key):
        _, p, t = key
        if (CTX, t) not in begun:
            begun.add((CTX, t))
            for h in range(3):
                for side in (0, 1):
                    only(reach(side, h), lambda: wait((CTX, side + 2, t, h), lanes(t, source(side, h) * 2 + 1 - c)))
            wait((CTX, 4, t, 0), lanes(t, j * 2 + 1 - c))
        here = pl.ds(t * ROWS, ROWS)
        ks = [plane(dy) for dy in PLANES[p]]
        lhs = [cbuf[:, here, pl.ds(pl.multiple_of(k * 384, 128), 384)].reshape(8 * ROWS, 384) for k in ks]
        rhs = [wbuf[pl.ds(pl.multiple_of(k * 8, 8), 8), 0:48, :].reshape(384, 768) for k in ks]
        product = jnp.dot(
            jnp.concatenate(lhs, axis=1), jnp.concatenate(rhs, axis=0), preferred_element_type=jnp.float32
        )
        if (UNIT, t) in begun:
            acc[t] += product
        else:
            begun.add((UNIT, t))
            acc[t] = product

    def project(key):
        t = key[1]
        here = pl.ds(t * ROWS, ROWS)
        if PROJ not in begun:
            begun.add(PROJ)
            loads[4].wait()
        gain = gain_ref[...].astype(jnp.float32).reshape(1, 768)
        stream = (res_ref[:, here, :].reshape(8 * ROWS, 768).astype(jnp.float32) + acc[t]).astype(jnp.bfloat16)
        value = stream.astype(jnp.float32)
        total = jnp.sum(value, axis=1, keepdims=True)
        squares = jnp.sum(value * value, axis=1, keepdims=True)
        scaled = (value * gain).astype(jnp.bfloat16)
        mapped = lax.dot_general(scaled, down[...], (((1,), (1,)), ((), ())), preferred_element_type=jnp.float32)
        column = lax.broadcasted_iota(jnp.int32, (8 * ROWS, 128), 1)
        stats = jnp.where(column == 0, total, jnp.where(column == 1, squares, 0.0))
        for k in range(8):
            cut = slice(k * ROWS, (k + 1) * ROWS)
            part[t, k % 2, k // 2] = mapped[cut]
            columns[k, here, :] = stats[cut]
        begun.add((PROJ, t))
        send((PAIR, t), lambda: (part.at[t, 1 - c], pair.at[t], sibling))
        if all((PROJ, k) in begun for k in range(CHUNKS)):
            stats_start(gain)

    def stats_start(gain):
        rows = jnp.broadcast_to(gain, (16, 768)).astype(jnp.bfloat16)
        shares = lax.dot_general(rows, down[...], (((1,), (1,)), ((), ())), preferred_element_type=jnp.float32)
        row = lax.broadcasted_iota(jnp.int32, (8, 128), 0)
        lower = jnp.zeros((8, 128), jnp.float32)
        for i in range(6):
            lower = jnp.where(row == i + 2, shares[0:8, i * 128:(i + 1) * 128], lower)
        for k in range(8):
            tiles[k % 2, k // 2] = jnp.where(row < 2, jnp.transpose(columns[k])[0:8, :], lower)
        send((STAT, 0), lambda: (tiles.at[1 - c], tiles_in, sibling))

    def stats_pass():
        wait((STAT, 0), tiles_in)
        tiles_sum[...] = tiles[c] + tiles_in[...]
        for d in (2, 1, 3):
            send((STAT, d), lambda d=d: (tiles_sum.at[(j + d) % 4], tiles_far.at[d - 1], chip_dev[d - 1]))

    def stats_end():
        total = tiles_sum[j]
        for d in (2, 1, 3):
            wait((STAT, d), tiles_far.at[d - 1])
            total = total + tiles_far[d - 1]
        return jnp.transpose(jnp.concatenate([total, jnp.zeros((120, 128), jnp.float32)], axis=0)), jnp.concatenate(
            [total[i + 2:i + 3, :] for i in range(6)], axis=1
        )

    def piece(ref, t, dest):
        return ref.at[t, dest]

    def add_pair(key):
        t = key[1]
        wait(key, pair.at[t])
        line[t] = part[t, c] + pair[t]
        for i in range(3):
            pass_on(t, 0, 0, 3 - i, True)
            pass_on(t, 3, 1, i, True)
        begun.add(key)
        if all((PAIR, k) in begun for k in range(CHUNKS)):
            stats_pass()

    def pass_on(t, chip, side, dest, first=False):
        kind, arrived = ((UP, up_in), (DOWN, down_in))[side]
        if not first:

            def add():
                wait((kind, t, dest), piece(arrived, t, dest))
                line[t, dest] += arrived[t, dest]

            only((chip,), add)
        send((kind, t, dest), lambda: (piece(line, t, dest), piece(arrived, t, dest), z_dev[side]), (chip,))

    def finish(key):
        t = key[1]
        for chip in range(4):

            def add():
                total = line[t, chip]
                if chip > 0:
                    wait((UP, t, chip), piece(up_in, t, chip))
                    total = total + up_in[t, chip]
                if chip < 3:
                    wait((DOWN, t, chip), piece(down_in, t, chip))
                    total = total + down_in[t, chip]
                sums[t * ROWS:(t + 1) * ROWS, :] = total

            only((chip,), add)

    def task(key):
        kind = key[0]
        if kind == Z:
            z_event(key)
        elif kind in (O, PD):
            (y_first if key[1] else x_second)(key)
        elif kind == PW:
            (y_second if key[1] else x_first)(key)
        elif kind == CTX:
            ctx_event(key)
        elif kind == P1:
            _, t, i = key
            pass_on(t, 1, 0, 3 - i)
            pass_on(t, 2, 1, i)
        elif kind == P2:
            pass_on(key[1], 2, 0, 3)
            pass_on(key[1], 1, 1, 0)
        else:
            {PICK: pick, UNIT: unit, PROJ: project, PAIR: add_pair, FIN: finish}[kind](key)

    def drain():
        for key, make, chips in sent:
            only(chips, lambda: remote(key, *make()).wait_send())
        sent.clear()

    def side_block():
        for load in loads[5:]:
            load.wait()
        stats, gain_map = stats_end()
        mean = stats[:, 0:1] * (1.0 / (8 * 768))
        spread = stats[:, 1:2] * (1.0 / (8 * 768)) - mean * mean
        scale = 1.0 / jnp.sqrt(spread + 1e-06)
        first = (sums[0:128, 0:384] - mean * gain_map[:, 0:384]) * scale
        second = (sums[0:128, 384:768] - mean * gain_map[:, 384:768]) * scale
        bend, f_slope = gelu_and_slope(exact_dot(second, f_ref[...], 0))
        upper = first + bend
        bend, g_slope = gelu_and_slope(exact_dot(upper, g_ref[...], 0))
        lower = second + bend
        o_ref[:, 0:384] = upper
        o_ref[:, 384:768] = lower
        back = (lower - targets_ref[:, 384:768]) * (1.0 / TOKENS) * g_slope
        upper_total = (upper - targets_ref[:, 0:384]) * (1.0 / TOKENS) + exact_dot(back, g_ref[...], 1)
        whole = lax.Precision.HIGHEST
        over_tokens = (((0,), (0,)), ((), ()))
        grads[1] = lax.dot_general(upper, back, over_tokens, precision=whole, preferred_element_type=jnp.float32)
        grads[0] = lax.dot_general(second, upper_total * f_slope, over_tokens, precision=whole, preferred_element_type=jnp.float32)

    def rows_of(ref, at, count):
        return ref.at[pl.ds(pl.multiple_of(at * count, 8), count)]

    def owned(at, h):
        return pl.ds(pl.multiple_of(at * 48 + 24 * h, 8), 24)

    def third(at, h):
        return (at >= 3 * h) & (at < 3 * h + 3)

    def reducer():
        return pos_b < 6

    def there(h, d, core, far):
        base = far * y + (1 - far) * z
        return fin.at[core, owned((base + 8 - d) % 8, h)]

    def gradient_sum():
        send((GRAD, 0), lambda: (grads.at[1 - c], buf0, sibling))
        wait((GRAD, 0), buf0)
        summed[...] = grads[c] + buf0[...]
        for h in (0, 1):
            for d in FAR_FIRST:
                send((GRAD, 1, h, d), lambda h=h, d=d: (summed.at[owned((pos_a + d) % 8, h)], buf_a.at[h, d - 1], along_a(d)))
        earlier, later = sent[:-15], sent[-15:]
        sent[:] = earlier
        drain()
        sent.extend(later)
        for h in (0, 1):
            total = summed[owned(pos_a, h), :]
            for d in FAR_FIRST:
                wait((GRAD, 1, h, d), buf_a.at[h, d - 1])
                total = total + buf_a[h, d - 1]
            mid[24 * h:24 * h + 24, :] = total
            for d in FAR_FIRST:
                send(
                    (GRAD, 2, d),
                    lambda d=d: (rows_of(mid, (pos_b + d) % 8, 8), buf_b.at[d - 1], along_b(d)),
                    lambda d=d, h=h: third((pos_b + d) % 8, h),
                )

        def reduce():
            total = mid[pl.ds(pl.multiple_of(pos_b * 8, 8), 8), :]
            for d in FAR_FIRST:
                wait((GRAD, 2, d), buf_b.at[d - 1])
                total = total + buf_b[d - 1]
            buf_x[x] = total

        only(reducer, reduce)
        for d in (2, 1, 3):
            send((GRAD, 3, d), lambda d=d: (buf_x.at[x], buf_x.at[x], along_x(d)), reducer)

        def cross():
            for d in (2, 1, 3):
                wait((GRAD, 3, d), buf_x.at[(x + 4 - d) % 4])
            tail[pl.ds(pl.multiple_of(pos_b * 8, 8), 8), :] = (buf_x[0] + buf_x[1]) + (buf_x[2] + buf_x[3])

        only(reducer, cross)
        for d in FAR_FIRST:
            send((GRAD, 4, d), lambda d=d: (rows_of(tail, pos_b, 8), rows_of(tail, pos_b, 8), along_b(d)), reducer)
        for h in (0, 1):
            for d in NEAR_FIRST:
                owner = (pos_b + 8 - d) % 8
                only(lambda: third(owner, h), lambda: wait((GRAD, 4, d), rows_of(tail, owner, 8)))
            for d in FAR_FIRST:
                send((GRAD, 5, h, d), lambda h=h, d=d: (tail.at[pl.ds(24 * h, 24)], fin.at[c, owned(pos_a, h)], along_a(d)))
            send((GRAD, 6, h, 0), lambda h=h: (tail.at[pl.ds(24 * h, 24)], fin.at[c, owned(pos_a, h)], sibling))
            fin[c, owned(pos_a, h), :] = tail[24 * h:24 * h + 24, :]
        for h in (0, 1):
            for d in NEAR_FIRST:
                wait((GRAD, 5, h, d), there(h, d, c, c))
                send((GRAD, 6, h, d), lambda h=h, d=d: (there(h, d, c, c), there(h, d, c, c), sibling))
        for h in (0, 1):
            for d in (0,) + NEAR_FIRST:
                wait((GRAD, 6, h, d), there(h, d, 1 - c, 1 - c))
        f_out[...] = fin[0]
        g_out[...] = fin[1]

    send((Z,), lambda: (pack_ref, block(O, 0, 0), z_far))
    for s in (0, 1):
        send_block((O, 1, 0, 1, s), O, 0, 0, y_dev[s])
    start_x(O, 0)
    for t in range(CHUNKS):
        own_ctx(t, 0, (0, 1, 2) if t < LEAD else (0,))
        own_ctx(t, 1, (1, 2, 3) if t < LEAD else (3,))
    for t in range(CHUNKS):
        send((CTX, 4, t, 0), lambda t=t: (mine(t), lanes(t, n), sibling))
    for copy in keep():
        copy.start()
    for key in ORDER:
        task(key)
    side_block()
    gradient_sum()
    drain()


def fused(context, out_weight, side_down, ln_gain, residual, f_weight, g_weight, targets):
    vmem = pl.BlockSpec(memory_space=pltpu.VMEM)
    away = pl.BlockSpec(memory_space=pltpu.HBM)
    f32 = jnp.float32
    bf16 = jnp.bfloat16
    piece = pltpu.VMEM((CHUNKS, 4, ROWS, WIDTH), f32)
    square = jax.ShapeDtypeStruct((384, 384), f32)
    return pl.pallas_call(
        fused_kernel,
        out_shape=(jax.ShapeDtypeStruct((128, 768), f32), square, square),
        in_specs=[away] * 8,
        out_specs=(vmem, vmem, vmem),
        scratch_shapes=[
            pltpu.VMEM((8, 128, 384), bf16),
            pltpu.VMEM((48, 768), bf16),
            pltpu.VMEM((12, 768), bf16),
            pltpu.VMEM((768,), bf16),
            pltpu.VMEM((64, 768), bf16),
            pltpu.VMEM((8, 128, 768), bf16),
            pltpu.VMEM((384, 384), bf16),
            pltpu.VMEM((384, 384), bf16),
            pltpu.VMEM((128, 768), f32),
            pltpu.VMEM((64, 64, 768), bf16),
            pltpu.VMEM((8, 128, 3072), bf16),
            pltpu.VMEM((768, 768), bf16),
            pltpu.VMEM((CHUNKS, 8 * ROWS, 768), f32),
            pltpu.VMEM((CHUNKS, 2, 4, ROWS, WIDTH), f32),
            piece,
            piece,
            piece,
            piece,
            pltpu.VMEM((128, WIDTH), f32),
            pltpu.VMEM((8, 128, 128), f32),
            pltpu.VMEM((2, 4, 8, 128), f32),
            pltpu.VMEM((4, 8, 128), f32),
            pltpu.VMEM((4, 8, 128), f32),
            pltpu.VMEM((3, 8, 128), f32),
            pltpu.VMEM((2, 384, 384), f32),
            pltpu.VMEM((384, 384), f32),
            pltpu.VMEM((384, 384), f32),
            pltpu.VMEM((2, 7, 24, 384), f32),
            pltpu.VMEM((48, 384), f32),
            pltpu.VMEM((7, 8, 384), f32),
            pltpu.VMEM((4, 8, 384), f32),
            pltpu.VMEM((48, 384), f32),
            pltpu.VMEM((2, 384, 384), f32),
            pltpu.SemaphoreType.DMA((10,)),
            pltpu.SemaphoreType.DMA((SLOTS,)),
            pltpu.SemaphoreType.DMA((SLOTS,)),
        ],
        compiler_params=pltpu.CompilerParams(collective_id=0, has_side_effects=True, vmem_limit_bytes=60 * 1024 * 1024),
        name="fused_layer",
    )(
        context.reshape(8, 128, 384), out_weight, side_down.T, ln_gain, residual.reshape(8, 128, 768),
        f_weight, g_weight, targets,
    )


def hand_over(a_ref, b_ref, c_ref, a_out, b_out, c_out, a_kept, b_kept, c_kept, sems):
    steps = [
        (pltpu.make_async_copy(src, kept, sems.at[0, i]), pltpu.make_async_copy(kept, dst, sems.at[1, i]))
        for i, (src, kept, dst) in enumerate(
            ((a_ref, a_kept, a_out), (b_ref, b_kept, b_out), (c_ref, c_kept, c_out))
        )
    ]
    for load, _ in steps:
        load.start()
    for load, store in steps:
        load.wait()
        store.start()
    for _, store in steps:
        store.wait()


def per_device(context, out_weight, residual, ln_gain, side_down, f_weight, g_weight, targets):
    results = fused(context, out_weight, side_down, ln_gain, residual, f_weight, g_weight, targets)
    away = pl.BlockSpec(memory_space=pltpu.HBM)
    return pl.pallas_call(
        hand_over,
        out_shape=tuple(jax.ShapeDtypeStruct(r.shape, r.dtype) for r in results),
        in_specs=[away] * 3,
        out_specs=(away,) * 3,
        scratch_shapes=[pltpu.VMEM(r.shape, r.dtype) for r in results] + [pltpu.SemaphoreType.DMA((2, 3))],
        name="hand_over",
    )(*results)


def solution(mesh):
    in_specs = (
        P("wide", "narrow"),
        P("wide", "narrow"),
        P("wide", "narrow"),
        P("narrow"),
        P("narrow", "wide"),
        P(),
        P(),
        P(("wide", "narrow"), None),
    )
    out_specs = (P(("wide", "narrow"), None), P(), P())
    return jax.shard_map(
        per_device, mesh=mesh, in_specs=in_specs, out_specs=out_specs, check_vma=False
    )
```
